32 devices in a mesh: grp: 2 (over core), blk: 16 (over z, y, x).
Axes of the slice: x: 2, y: 2, z: 4, core: 2. Of those that a mesh axis runs over, the one named last changes fastest.
Arguments:
- nullspace: float32 [6, 65536], P(None, ('grp', 'blk')), may hold values from -6 to 6
- agg_ids: int32 [65536], P(('grp', 'blk')), may hold values from 0 to 1535
- nbr_index: int32 [8, 65536], P(None, ('grp', 'blk')), may hold values from 0 to 6143
- nbr_weight: float32 [8, 65536], P(None, ('grp', 'blk')), may hold values from -0.25 to 0.25
Outputs:
- factor: float32 [21, 3072], P(None, ('grp', 'blk'))
- spread: float32 [3072], P(('grp', 'blk'))
The draws below stay inside these ranges and needn't reach their ends.
All inputs are finite; a program needn't handle non-finite values.
Results may differ from the reference program's by a relative error of at most 0.000088.
Values sent between devices are 32-bit elements; how exact they have to be, the bound alone decides.
No kernel may reach another device: no remote copies, remote signals or barrier semaphores. Data moves between devices by JAX's collectives and lax.ppermute only.
A program may use at most 64 MiB of HBM per device.

```python
import jax
import jax.numpy as jnp
from jax import lax

NULL = 6
NEIGH = 8
ROWS_DEV = 2048
AGG_DEV = 96
ROWS_ALL = 65536
AGG = 1536
AGGS = 3072
N_GRP = 2
N_BLK = 16


def touch_ends(entries, stream_key, smallest, high):
    longest = entries.shape.index(max(entries.shape))
    spots = []
    for shift in (0, 1):
        where = [jax.random.randint(jax.random.fold_in(stream_key, axis), (), 0, length) for axis, length in enumerate(entries.shape)]
        where[longest] = (where[longest] + shift) % entries.shape[longest]
        spots.append(tuple(where))
    return entries.at[spots[0]].set(smallest).at[spots[1]].set(high)


def level_of(stream_key, extent, pieces, smallest, largest):
    factor_of, own = 1.0, jax.random.fold_in(stream_key, 6)
    for dim, parts in pieces:
        heights = jnp.exp(jax.random.uniform(jax.random.fold_in(own, dim), (parts,), jnp.float32, smallest / len(pieces), largest / len(pieces)))
        factor_of = factor_of * jnp.repeat(heights, extent[dim] // parts).reshape([-1 if axis == dim else 1 for axis in range(len(extent))])
    return factor_of


def gaussian(own_key, dims, deviation, most, shards=(), held_as=jnp.bfloat16):
    result = jax.random.normal(own_key, dims, jnp.float32) * deviation
    if len(shards) > 0:
        result = level_of(own_key, dims, shards, -0.22, 0.18) * result
    return jnp.clip(result, min=-most, max=most).astype(held_as)


def setup_inputs(seed: int = 0) -> dict:
    splits = jax.random.split(jax.random.key(seed), 5)
    nullspace = gaussian(splits[0], (NULL, ROWS_ALL), 1.0, 6.0, ((1, 32),), jnp.float32)
    agg_ids = touch_ends(jax.random.randint(splits[1], (ROWS_ALL,), 0, AGG), jax.random.fold_in(splits[1], 1), 0, AGG - 1).astype(jnp.int32)
    nbr_index = touch_ends(jax.random.randint(splits[2], (NEIGH, ROWS_ALL), 0, 3 * ROWS_DEV), jax.random.fold_in(splits[2], 1), 0, (3 * ROWS_DEV) - 1).astype(jnp.int32)
    nbr_weight = jnp.clip(jax.random.uniform(splits[3], (NEIGH, ROWS_ALL), jnp.float32, -0.25, 0.25) * level_of(splits[3], (NEIGH, ROWS_ALL), ((1, 32),), -0.4, 0.0), -0.25, 0.25)
    return {"nullspace": nullspace, "agg_ids": agg_ids, "nbr_index": nbr_index, "nbr_weight": nbr_weight}


def pair_list():
    return [(p, q) for p in range(6) for q in range(p, 6)]

def factorize(packed):
    pairs = pair_list()
    entry = {}
    for idx, (p, q) in enumerate(pairs):
        entry[p, q] = packed[idx]
        entry[q, p] = packed[idx]
    lower = {}
    for j in range(6):
        total = entry[j, j]
        for k in range(j):
            total = total - lower[j, k] * lower[j, k]
        diag = jnp.sqrt(total)
        lower[j, j] = diag
        for i in range(j + 1, 6):
            total = entry[i, j]
            for k in range(j):
                total = total - lower[i, k] * lower[j, k]
            lower[i, j] = total / diag
    factor = jnp.stack([lower[q, p] for p, q in pairs], axis=0)
    diags = jnp.stack([lower[j, j] for j in range(6)], axis=0)
    spread = jnp.log(lax.optimization_barrier(jnp.max(diags, axis=0))) - jnp.log(lax.optimization_barrier(jnp.min(diags, axis=0)))
    return (factor, spread)

def reference(nullspace, agg_ids, nbr_index, nbr_weight):
    grid = nullspace.reshape(NULL, N_GRP, N_BLK, ROWS_DEV)
    zero_row = jnp.zeros((NULL, 1, N_BLK, ROWS_DEV), jnp.float32)
    previous = jnp.concatenate([zero_row, grid[:, :-1]], axis=1)
    following = jnp.concatenate([grid[:, 1:], zero_row], axis=1)
    extended = jnp.concatenate([previous, grid, following], axis=3)
    index = nbr_index.reshape(NEIGH, N_GRP, N_BLK, ROWS_DEV)
    weight = nbr_weight.reshape(NEIGH, N_GRP, N_BLK, ROWS_DEV)
    smoothed = grid
    for k in range(NEIGH):
        picked = jnp.take_along_axis(extended, jnp.broadcast_to(index[k][None], (NULL, N_GRP, N_BLK, ROWS_DEV)), axis=3)
        smoothed = smoothed - weight[k][None] * picked
    smoothed = smoothed.reshape(NULL, ROWS_ALL)
    terms = jnp.stack([smoothed[p] * smoothed[q] for p, q in pair_list()], axis=0)
    group_of = (jnp.arange(ROWS_ALL, dtype=jnp.int32) // (ROWS_DEV * N_BLK)).astype(jnp.int32)
    global_ids = (group_of * AGG + agg_ids).astype(jnp.int32)
    summed = jax.ops.segment_sum(terms.T, global_ids, num_segments=AGGS).T
    identity = jnp.array([1.0 if p == q else 0.0 for p, q in pair_list()], jnp.float32)
    gram = summed * (AGG_DEV / ROWS_DEV) + identity[:, None]
    return factorize(gram)
```

```python
import functools

import jax
import jax.numpy as jnp
from jax import lax
from jax.experimental import pallas as pl
from jax.experimental.pallas import tpu as pltpu
from jax.sharding import PartitionSpec as P

ROWS_DEV = 2048
AGG_DEV = 96
LANES = 128


def pair_list(vectors):
    return [(p, q) for p in range(vectors) for q in range(p, vectors)]


def share_of(ids, shares):
    shift = 22
    factor = -(-(1 << shift) // AGG_DEV)
    most = shares * AGG_DEV - 1
    assert most * factor < 2**31 and (factor * AGG_DEV - (1 << shift)) * most < (1 << shift)
    return lax.shift_right_logical(ids * factor, shift)


def gram_kernel(shares, own_ref, *refs):
    *others, ids_ref, index_ref, weight_ref, out_ref = refs
    vectors, rows = own_ref.shape
    pairs = pair_list(vectors)
    padded = out_ref.shape[1]
    tables = [(own_ref, rows)]
    for table_ref, start_ref in zip(others[0::2], others[1::2]):
        tables.append((table_ref, start_ref[0]))
    gram = [jnp.zeros((shares * padded, AGG_DEV), jnp.float32) for _ in range(2)]
    step = 2 * LANES
    for first in range(0, rows, step):
        pieces = []
        for start in range(first, first + step, LANES):
            here = slice(start, start + LANES)
            index = index_ref[:, here]
            weight = weight_ref[:, here]
            low = jnp.bitwise_and(index, LANES - 1)
            picked = [jnp.zeros(index.shape, jnp.float32) for _ in range(vectors)]
            for table_ref, base in tables:
                high = lax.shift_right_arithmetic(index - base, 7)
                for chunk in range(rows // LANES):
                    found = high == chunk
                    for v in range(vectors):
                        row = table_ref[v : v + 1, chunk * LANES : (chunk + 1) * LANES]
                        value = jnp.take_along_axis(
                            jnp.broadcast_to(row, index.shape), low, axis=1, mode="promise_in_bounds"
                        )
                        picked[v] = jnp.where(found, value, picked[v])
            smooth = [
                own_ref[v : v + 1, here] - jnp.sum(weight * picked[v], axis=0, keepdims=True)
                for v in range(vectors)
            ]
            pieces.append([smooth[p] * smooth[q] for p, q in pairs])
        zero = jnp.zeros((padded - len(pairs), step), jnp.float32)
        terms = jnp.concatenate(
            [jnp.concatenate([half[i] for half in pieces], axis=1) for i in range(len(pairs))] + [zero],
            axis=0,
        )
        coarse = terms.astype(jnp.bfloat16).astype(jnp.float32)
        ids = ids_ref[:, first : first + step]
        share = share_of(ids, shares)
        within = ids - share * AGG_DEV
        lanes = lax.broadcasted_iota(jnp.int32, (AGG_DEV, step), 0)
        one_hot = (lanes == within).astype(jnp.float32).astype(jnp.bfloat16)
        for piece, part in enumerate((coarse, terms - coarse)):
            spread_out = jnp.concatenate(
                [jnp.where(share == s, part, 0.0) for s in range(shares)], axis=0
            ).astype(jnp.bfloat16)
            gram[piece] = gram[piece] + lax.dot_general(
                spread_out, one_hot, (((1,), (1,)), ((), ())), preferred_element_type=jnp.float32
            )
    out_ref[...] = (gram[0] + gram[1]).reshape(out_ref.shape)


def factor_kernel(vectors, parts_ref, factor_ref, spread_ref):
    pairs = pair_list(vectors)
    total = parts_ref[0]
    for source in range(1, parts_ref.shape[0]):
        total = total + parts_ref[source]
    entry = {}
    for i, (p, q) in enumerate(pairs):
        value = total[i : i + 1] * (AGG_DEV / ROWS_DEV)
        entry[p, q] = value + 1.0 if p == q else value
    upper = {}
    for j in range(vectors):
        pivot = entry[j, j]
        for k in range(j):
            pivot = pivot - upper[k, j] * upper[k, j]
        upper[j, j] = jnp.sqrt(pivot)
        for i in range(j + 1, vectors):
            rest = entry[j, i]
            for k in range(j):
                rest = rest - upper[k, i] * upper[k, j]
            upper[j, i] = rest / upper[j, j]
    for i, pair in enumerate(pairs):
        factor_ref[i : i + 1, :] = upper[pair]
    most = functools.reduce(jnp.maximum, [upper[j, j] for j in range(vectors)])
    least = functools.reduce(jnp.minimum, [upper[j, j] for j in range(vectors)])
    spread_ref[...] = jnp.log(most) - jnp.log(least)


def shards(nullspace, agg_ids, nbr_index, nbr_weight):
    vectors, rows = nullspace.shape
    groups, shares = lax.axis_size("grp"), lax.axis_size("blk")
    pairs = pair_list(vectors)
    padded = -(-len(pairs) // 8) * 8
    vmem = pl.BlockSpec(memory_space=pltpu.VMEM)
    smem = pl.BlockSpec(memory_space=pltpu.SMEM)
    if groups == 2:
        other = lax.ppermute(nullspace, "grp", [(0, 1), (1, 0)])
        start = (2 * rows * (1 - lax.axis_index("grp"))).astype(jnp.int32).reshape(1)
        tables = [other, start]
    else:
        before = lax.ppermute(nullspace, "grp", [(i, i + 1) for i in range(groups - 1)])
        after = lax.ppermute(nullspace, "grp", [(i + 1, i) for i in range(groups - 1)])
        tables = [
            before,
            jnp.zeros((1,), jnp.int32),
            after,
            jnp.full((1,), 2 * rows, jnp.int32),
        ]
    partial = pl.pallas_call(
        functools.partial(gram_kernel, shares),
        out_shape=jax.ShapeDtypeStruct((shares, padded, AGG_DEV), jnp.float32),
        in_specs=[vmem] + [vmem, smem] * (len(tables) // 2) + [vmem] * 3,
        out_specs=vmem,
        name="gram",
    )(nullspace, *tables, agg_ids.reshape(1, rows), nbr_index, nbr_weight)
    parts = lax.all_to_all(partial, "blk", 0, 0, tiled=True)
    factor, spread = pl.pallas_call(
        functools.partial(factor_kernel, vectors),
        out_shape=(
            jax.ShapeDtypeStruct((len(pairs), AGG_DEV), jnp.float32),
            jax.ShapeDtypeStruct((1, AGG_DEV), jnp.float32),
        ),
        in_specs=[vmem],
        out_specs=(vmem, vmem),
        name="factor",
    )(parts)
    return factor, spread.reshape(AGG_DEV)


def solution(mesh):
    return jax.shard_map(
        shards,
        mesh=mesh,
        in_specs=(
            P(None, ("grp", "blk")),
            P(("grp", "blk")),
            P(None, ("grp", "blk")),
            P(None, ("grp", "blk")),
        ),
        out_specs=(P(None, ("grp", "blk")), P(("grp", "blk"))),
        check_vma=False,
    )
```

```python
import functools

import jax
import jax.numpy as jnp
from jax import lax
from jax.experimental import pallas as pl
from jax.experimental.pallas import tpu as pltpu
from jax.sharding import PartitionSpec as P

ROWS_DEV = 2048
AGG_DEV = 96
LANES = 128
NULL_MOST = 6.0
SPLIT = 11
SCALE_WHOLE = (2.0 ** (31 - SPLIT) - 1.0) / NULL_MOST
SCALE_SPLIT = (2.0 ** (2 * SPLIT - 1) - 1.0) / NULL_MOST
KEEP = (1 << SPLIT) - 1


def pair_list(vectors):
    return [(p, q) for p in range(vectors) for q in range(p, vectors)]


def share_of(ids, shares):
    shift = 22
    factor = -(-(1 << shift) // AGG_DEV)
    most = shares * AGG_DEV - 1
    assert most * factor < 2**31 and (factor * AGG_DEV - (1 << shift)) * most < (1 << shift)
    return lax.shift_right_logical(ids * factor, shift)


def encode(table):
    words = 2 * table.shape[0] // 3
    whole = jnp.round(table[:words] * SCALE_WHOLE).astype(jnp.int32)
    split = jnp.round(table[words:] * SCALE_SPLIT).astype(jnp.int32)
    lower = [
        jnp.bitwise_and(split[r // 2 : r // 2 + 1] >> (0 if r % 2 else SPLIT), KEEP) for r in range(words)
    ]
    return jnp.bitwise_or(whole << SPLIT, jnp.concatenate(lower, axis=0))


def decode(words):
    values = [(word >> SPLIT).astype(jnp.float32) for word in words]
    for upper, lower in zip(words[0::2], words[1::2]):
        split = jnp.bitwise_or((upper << (32 - SPLIT)) >> (32 - 2 * SPLIT), jnp.bitwise_and(lower, KEEP))
        values.append(split.astype(jnp.float32))
    return values


def pick(picked, index, tables):
    low = jnp.bitwise_and(index, LANES - 1)
    for table_ref, base in tables:
        high = lax.shift_right_arithmetic(index - base, LANES.bit_length() - 1)
        for chunk in range(table_ref.shape[1] // LANES):
            found = high == chunk
            for word in range(len(picked)):
                row = table_ref[word : word + 1, chunk * LANES : (chunk + 1) * LANES]
                value = jnp.take_along_axis(
                    jnp.broadcast_to(row, index.shape), low, axis=1, mode="promise_in_bounds"
                )
                picked[word] = jnp.where(found, value, picked[word])
    return picked


def own_kernel(*refs):
    arguments, copies = refs[:4], refs[4:8]
    picked_ref, table_ref, sems = refs[8:]
    rows = copies[0].shape[1]
    moves = [
        pltpu.make_async_copy(source, target, sems.at[i])
        for i, (source, target) in enumerate(zip(arguments, copies))
    ]
    for move in moves:
        move.start()
    own_ref, index_ref = copies[:2]
    moves[0].wait()
    table_ref[...] = encode(own_ref[...])
    moves[1].wait()
    for start in range(0, rows, LANES):
        here = slice(start, start + LANES)
        index = index_ref[:, here]
        zero = [jnp.zeros(index.shape, jnp.int32) for _ in range(table_ref.shape[0])]
        for word, value in enumerate(pick(zero, index, [(table_ref, rows)])):
            picked_ref[word, :, here] = value
    moves[2].wait()
    moves[3].wait()


def gram_kernel(shares, count, *refs):
    own_ref, index_ref, weight_ref, ids_ref, picked_ref = refs[:5]
    others, starts = refs[5 : 5 + count], refs[5 + count : 5 + 2 * count]
    out_ref, *table_refs = refs[5 + 2 * count :]
    vectors, rows = own_ref.shape
    pairs = pair_list(vectors)
    padded = out_ref.shape[1]
    tables = []
    for other_ref, start_ref, table_ref in zip(others, starts, table_refs):
        table_ref[...] = encode(other_ref[...])
        tables.append((table_ref, start_ref[0]))
    words = picked_ref.shape[0]
    scales = [1.0 / SCALE_WHOLE] * words + [1.0 / SCALE_SPLIT] * (vectors - words)
    gram = [jnp.zeros((shares * padded, AGG_DEV), jnp.float32) for _ in range(2)]
    step = 2 * LANES
    for first in range(0, rows, step):
        pieces = []
        for start in range(first, first + step, LANES):
            here = slice(start, start + LANES)
            weight = weight_ref[:, here]
            picked = pick([picked_ref[word, :, here] for word in range(words)], index_ref[:, here], tables)
            smooth = [
                own_ref[v : v + 1, here] - jnp.sum(weight * value, axis=0, keepdims=True) * scales[v]
                for v, value in enumerate(decode(picked))
            ]
            pieces.append([smooth[p] * smooth[q] for p, q in pairs])
        zero = jnp.zeros((padded - len(pairs), step), jnp.float32)
        terms = jnp.concatenate(
            [jnp.concatenate([half[i] for half in pieces], axis=1) for i in range(len(pairs))] + [zero],
            axis=0,
        )
        coarse = terms.astype(jnp.bfloat16).astype(jnp.float32)
        ids = ids_ref[:, first : first + step]
        share = share_of(ids, shares)
        within = ids - share * AGG_DEV
        lanes = lax.broadcasted_iota(jnp.int32, (AGG_DEV, step), 0)
        one_hot = (lanes == within).astype(jnp.float32).astype(jnp.bfloat16)
        for piece, part in enumerate((coarse, terms - coarse)):
            spread_out = jnp.concatenate(
                [jnp.where(share == s, part, 0.0) for s in range(shares)], axis=0
            ).astype(jnp.bfloat16)
            gram[piece] = gram[piece] + lax.dot_general(
                spread_out, one_hot, (((1,), (1,)), ((), ())), preferred_element_type=jnp.float32
            )
    out_ref[...] = (gram[0] + gram[1]).reshape(out_ref.shape)


def factor_kernel(vectors, parts_ref, factor_ref, spread_ref):
    pairs = pair_list(vectors)
    total = parts_ref[0]
    for source in range(1, parts_ref.shape[0]):
        total = total + parts_ref[source]
    entry = {}
    for i, (p, q) in enumerate(pairs):
        value = total[i : i + 1] * (AGG_DEV / ROWS_DEV)
        entry[p, q] = value + 1.0 if p == q else value
    upper = {}
    for j in range(vectors):
        pivot = entry[j, j]
        for k in range(j):
            pivot = pivot - upper[k, j] * upper[k, j]
        upper[j, j] = jnp.sqrt(pivot)
        for i in range(j + 1, vectors):
            rest = entry[j, i]
            for k in range(j):
                rest = rest - upper[k, i] * upper[k, j]
            upper[j, i] = rest / upper[j, j]
    for i, pair in enumerate(pairs):
        factor_ref[i : i + 1, :] = upper[pair]
    most = functools.reduce(jnp.maximum, [upper[j, j] for j in range(vectors)])
    least = functools.reduce(jnp.minimum, [upper[j, j] for j in range(vectors)])
    spread_ref[...] = jnp.log(most) - jnp.log(least)


def shards(nullspace, agg_ids, nbr_index, nbr_weight):
    vectors, rows = nullspace.shape
    assert vectors % 3 == 0 and rows % (2 * LANES) == 0
    words = 2 * vectors // 3
    groups, shares = lax.axis_size("grp"), lax.axis_size("blk")
    pairs = pair_list(vectors)
    padded = -(-len(pairs) // 8) * 8
    vmem = pl.BlockSpec(memory_space=pltpu.VMEM)
    smem = pl.BlockSpec(memory_space=pltpu.SMEM)
    hbm = pl.BlockSpec(memory_space=pltpu.HBM)
    if groups == 2:
        others = [lax.ppermute(nullspace, "grp", [(0, 1), (1, 0)])]
        starts = [(2 * rows * (1 - lax.axis_index("grp"))).astype(jnp.int32).reshape(1)]
    else:
        others = [
            lax.ppermute(nullspace, "grp", [(i, i + 1) for i in range(groups - 1)]),
            lax.ppermute(nullspace, "grp", [(i + 1, i) for i in range(groups - 1)]),
        ]
        starts = [jnp.zeros((1,), jnp.int32), jnp.full((1,), 2 * rows, jnp.int32)]
    arguments = (nullspace, nbr_index, nbr_weight, agg_ids.reshape(1, rows))
    held = pl.pallas_call(
        own_kernel,
        out_shape=[jax.ShapeDtypeStruct(a.shape, a.dtype) for a in arguments]
        + [jax.ShapeDtypeStruct((words,) + nbr_index.shape, jnp.int32)],
        in_specs=[hbm] * 4,
        out_specs=[vmem] * 5,
        scratch_shapes=[pltpu.VMEM((words, rows), jnp.int32), pltpu.SemaphoreType.DMA((4,))],
        compiler_params=pltpu.CompilerParams(vmem_limit_bytes=4 << 20),
        cost_estimate=pl.CostEstimate(flops=1 << 22, bytes_accessed=1 << 18, transcendentals=0),
        name="own",
    )(*[pltpu.with_memory_space_constraint(a, pltpu.HBM) for a in arguments])
    partial = pl.pallas_call(
        functools.partial(gram_kernel, shares, len(others)),
        out_shape=jax.ShapeDtypeStruct((shares, padded, AGG_DEV), jnp.float32),
        in_specs=[vmem] * (5 + len(others)) + [smem] * len(others),
        out_specs=vmem,
        scratch_shapes=[pltpu.VMEM((words, rows), jnp.int32) for _ in others],
        compiler_params=pltpu.CompilerParams(vmem_limit_bytes=8 << 20),
        name="gram",
    )(*held, *others, *starts)
    parts = lax.all_to_all(partial, "blk", 0, 0, tiled=True)
    factor, spread = pl.pallas_call(
        functools.partial(factor_kernel, vectors),
        out_shape=(
            jax.ShapeDtypeStruct((len(pairs), AGG_DEV), jnp.float32),
            jax.ShapeDtypeStruct((1, AGG_DEV), jnp.float32),
        ),
        in_specs=[vmem],
        out_specs=(vmem, vmem),
        compiler_params=pltpu.CompilerParams(vmem_limit_bytes=4 << 20),
        name="factor",
    )(parts)
    return factor, spread.reshape(AGG_DEV)


def solution(mesh):
    return jax.shard_map(
        shards,
        mesh=mesh,
        in_specs=(
            P(None, ("grp", "blk")),
            P(("grp", "blk")),
            P(None, ("grp", "blk")),
            P(None, ("grp", "blk")),
        ),
        out_specs=(P(None, ("grp", "blk")), P(("grp", "blk"))),
        check_vma=False,
    )
```

```python
import functools

import jax
import jax.numpy as jnp
from jax import lax
from jax.experimental import pallas as pl
from jax.experimental.pallas import tpu as pltpu
from jax.sharding import PartitionSpec as P

ROWS_DEV = 2048
AGG_DEV = 96
LANES = 128
NULL_MOST = 6.0
SPLIT = 11
SCALE_WHOLE = (2.0 ** (31 - SPLIT) - 1.0) / NULL_MOST
SCALE_SPLIT = (2.0 ** (2 * SPLIT - 1) - 1.0) / NULL_MOST
KEEP = (1 << SPLIT) - 1


def pair_list(vectors):
    return [(p, q) for p in range(vectors) for q in range(p, vectors)]


def share_of(ids, shares):
    shift = 22
    factor = -(-(1 << shift) // AGG_DEV)
    most = shares * AGG_DEV - 1
    assert most * factor < 2**31 and (factor * AGG_DEV - (1 << shift)) * most < (1 << shift)
    return lax.shift_right_logical(ids * factor, shift)


def encode(table):
    words = 2 * table.shape[0] // 3
    whole = jnp.round(table[:words] * SCALE_WHOLE).astype(jnp.int32)
    split = jnp.round(table[words:] * SCALE_SPLIT).astype(jnp.int32)
    lower = [
        jnp.bitwise_and(split[r // 2 : r // 2 + 1] >> (0 if r % 2 else SPLIT), KEEP) for r in range(words)
    ]
    return jnp.bitwise_or(whole << SPLIT, jnp.concatenate(lower, axis=0))


def decode(words):
    values = [(word >> SPLIT).astype(jnp.float32) for word in words]
    for upper, lower in zip(words[0::2], words[1::2]):
        split = jnp.bitwise_or((upper << (32 - SPLIT)) >> (32 - 2 * SPLIT), jnp.bitwise_and(lower, KEEP))
        values.append(split.astype(jnp.float32))
    return values


def lane_pick(rows, low):
    return lax.gather(
        rows,
        low[:, :, None],
        lax.GatherDimensionNumbers(
            offset_dims=(),
            collapsed_slice_dims=(1,),
            start_index_map=(1,),
            operand_batching_dims=(0,),
            start_indices_batching_dims=(0,),
        ),
        slice_sizes=(1, 1),
        mode=lax.GatherScatterMode.PROMISE_IN_BOUNDS,
    )


def pick(picked, index, tables):
    low = jnp.bitwise_and(index, LANES - 1)
    for table_ref, base in tables:
        high = lax.shift_right_arithmetic(index - base, LANES.bit_length() - 1)
        for chunk in range(table_ref.shape[1] // LANES):
            found = high == chunk
            for word in range(len(picked)):
                row = table_ref[word : word + 1, chunk * LANES : (chunk + 1) * LANES]
                value = lane_pick(jnp.broadcast_to(row, index.shape), low)
                picked[word] = jnp.where(found, value, picked[word])
    return picked


def own_kernel(shares, *refs):
    arguments, copies = refs[:4], refs[4:8]
    picked_ref, column_ref, table_ref, sems = refs[8:]
    rows = copies[0].shape[1]
    moves = [
        pltpu.make_async_copy(source, target, sems.at[i])
        for i, (source, target) in enumerate(zip(arguments, copies))
    ]
    for move in moves:
        move.start()
    own_ref, index_ref, _, ids_ref = copies
    moves[0].wait()
    table_ref[...] = encode(own_ref[...])
    moves[1].wait()
    moves[3].wait()
    for start in range(0, rows, LANES):
        here = slice(start, start + LANES)
        index = index_ref[:, here]
        zero = [jnp.zeros(index.shape, jnp.int32) for _ in range(table_ref.shape[0])]
        for word, value in enumerate(pick(zero, index, [(table_ref, rows)])):
            picked_ref[word, :, here] = value
    moves[2].wait()


def to_wire(gram):
    tail = jnp.concatenate([gram[16:], jnp.zeros((8, LANES - AGG_DEV), gram.dtype)], axis=1)
    lanes = lax.broadcasted_iota(jnp.int32, (8, LANES), 1)
    rows = lax.broadcasted_iota(jnp.int32, (8, LANES), 0)
    out = []
    third = AGG_DEV // 3
    thirds = [pltpu.roll(tail, AGG_DEV - third * i, 1) for i in range(3)]
    for half in range(2):
        main = jnp.concatenate(
            [gram[8 * half : 8 * half + 8], jnp.zeros((8, LANES - AGG_DEV), gram.dtype)], axis=1
        )
        last = pltpu.roll(thirds[2], 5 - 3 * half, 0)
        side = jnp.where(rows < 5, thirds[half], last)
        out.append(jnp.where(lanes < AGG_DEV, main, side))
    return jnp.concatenate(out, axis=0)


def from_wire(wire):
    third = AGG_DEV // 3
    lanes = lax.broadcasted_iota(jnp.int32, (8, LANES), 1)
    rows = lax.broadcasted_iota(jnp.int32, (8, LANES), 0)
    first, second = wire[:8], wire[8:]
    last = jnp.where(rows < 3, pltpu.roll(first, 3, 0), pltpu.roll(second, 6, 0))
    thirds = [pltpu.roll(x, LANES - AGG_DEV + third * i, 1) for i, x in enumerate((first, second, last))]
    tail = jnp.where(lanes < third, thirds[0], jnp.where(lanes < 2 * third, thirds[1], thirds[2]))
    return jnp.concatenate([first, second, tail], axis=0)


def gram_kernel(shares, count, *refs):
    own_ref, index_ref, weight_ref, ids_ref, picked_ref, column_ref = refs[:6]
    others, starts = refs[6 : 6 + count], refs[6 + count : 6 + 2 * count]
    out_ref, *table_refs = refs[6 + 2 * count :]
    vectors, rows = own_ref.shape
    pairs = pair_list(vectors)
    padded = 24
    tables = []
    for other_ref, start_ref, table_ref in zip(others, starts, table_refs):
        table_ref[...] = encode(other_ref[...])
        tables.append((table_ref, start_ref[0]))
    words = picked_ref.shape[0]
    scales = [1.0 / SCALE_WHOLE] * words + [1.0 / SCALE_SPLIT] * (vectors - words)
    half_shares = shares // 2
    gram = [jnp.zeros((half_shares * 2 * padded, AGG_DEV), jnp.float32) for _ in range(2)]
    step = LANES
    for first in range(0, rows, step):
        pieces = []
        for start in range(first, first + step, LANES):
            here = slice(start, start + LANES)
            weight = weight_ref[:, here]
            picked = pick([picked_ref[word, :, here] for word in range(words)], index_ref[:, here], tables)
            smooth = [
                own_ref[v : v + 1, here] - jnp.sum(weight * value, axis=0, keepdims=True) * scales[v]
                for v, value in enumerate(decode(picked))
            ]
            pieces.append([smooth[p] * smooth[q] for p, q in pairs])
        zero = jnp.zeros((padded - len(pairs), step), jnp.float32)
        terms = jnp.concatenate(
            [jnp.concatenate([half[i] for half in pieces], axis=1) for i in range(len(pairs))] + [zero],
            axis=0,
        )
        coarse = terms.astype(jnp.bfloat16).astype(jnp.float32)
        both = jnp.concatenate([coarse, terms - coarse], axis=0)
        share = share_of(ids_ref[:, first : first + step], shares)
        ids = ids_ref[:, first : first + step]
        within = ids - share * AGG_DEV
        columns = lax.broadcasted_iota(jnp.int32, (AGG_DEV, step), 0)
        one_hot = (columns == within).astype(jnp.float32).astype(jnp.bfloat16)
        for half in range(2):
            masked = jnp.concatenate(
                [jnp.where(share == half * half_shares + s, both, 0.0) for s in range(half_shares)], axis=0
            ).astype(jnp.bfloat16)
            gram[half] = gram[half] + lax.dot_general(
                masked,
                one_hot,
                (((1,), (1,)), ((), ())),
                preferred_element_type=jnp.float32,
            )
    for half in range(2):
        for s in range(half_shares):
            at = 2 * padded * s
            out_ref[half * half_shares + s] = to_wire(
                gram[half][at : at + padded] + gram[half][at + padded : at + 2 * padded]
            )


def factor_kernel(vectors, parts_ref, factor_ref, spread_ref):
    pairs = pair_list(vectors)
    total = parts_ref[0]
    for source in range(1, parts_ref.shape[0]):
        total = total + parts_ref[source]
    total = from_wire(total)[:, :AGG_DEV]
    entry = {}
    for i, (p, q) in enumerate(pairs):
        value = total[i : i + 1] * (AGG_DEV / ROWS_DEV)
        entry[p, q] = value + 1.0 if p == q else value
    upper = {}
    for j in range(vectors):
        pivot = entry[j, j]
        for k in range(j):
            pivot = pivot - upper[k, j] * upper[k, j]
        upper[j, j] = jnp.sqrt(pivot)
        for i in range(j + 1, vectors):
            rest = entry[j, i]
            for k in range(j):
                rest = rest - upper[k, i] * upper[k, j]
            upper[j, i] = rest / upper[j, j]
    for i, pair in enumerate(pairs):
        factor_ref[i : i + 1, :] = upper[pair]
    most = functools.reduce(jnp.maximum, [upper[j, j] for j in range(vectors)])
    least = functools.reduce(jnp.minimum, [upper[j, j] for j in range(vectors)])
    spread_ref[...] = jnp.log(most) - jnp.log(least)


def shards(nullspace, agg_ids, nbr_index, nbr_weight):
    vectors, rows = nullspace.shape
    assert vectors % 3 == 0 and rows % (2 * LANES) == 0
    words = 2 * vectors // 3
    groups, shares = lax.axis_size("grp"), lax.axis_size("blk")
    pairs = pair_list(vectors)
    assert len(pairs) == 21 and shares % 2 == 0
    vmem = pl.BlockSpec(memory_space=pltpu.VMEM)
    smem = pl.BlockSpec(memory_space=pltpu.SMEM)
    hbm = pl.BlockSpec(memory_space=pltpu.HBM)
    if groups == 2:
        others = [lax.ppermute(nullspace, "grp", [(0, 1), (1, 0)])]
        starts = [(2 * rows * (1 - lax.axis_index("grp"))).astype(jnp.int32).reshape(1)]
    else:
        others = [
            lax.ppermute(nullspace, "grp", [(i, i + 1) for i in range(groups - 1)]),
            lax.ppermute(nullspace, "grp", [(i + 1, i) for i in range(groups - 1)]),
        ]
        starts = [jnp.zeros((1,), jnp.int32), jnp.full((1,), 2 * rows, jnp.int32)]
    arguments = (nullspace, nbr_index, nbr_weight, agg_ids.reshape(1, rows))
    held = pl.pallas_call(
        functools.partial(own_kernel, shares),
        out_shape=[jax.ShapeDtypeStruct(a.shape, a.dtype) for a in arguments]
        + [
            jax.ShapeDtypeStruct((words,) + nbr_index.shape, jnp.int32),
            jax.ShapeDtypeStruct((AGG_DEV, rows), jnp.bfloat16),
        ],
        in_specs=[hbm] * 4,
        out_specs=[vmem] * 6,
        scratch_shapes=[pltpu.VMEM((words, rows), jnp.int32), pltpu.SemaphoreType.DMA((4,))],
        compiler_params=pltpu.CompilerParams(vmem_limit_bytes=4 << 20),
        cost_estimate=pl.CostEstimate(flops=1 << 22, bytes_accessed=1 << 18, transcendentals=0),
        name="own",
    )(*[pltpu.with_memory_space_constraint(a, pltpu.HBM) for a in arguments])
    partial = pl.pallas_call(
        functools.partial(gram_kernel, shares, len(others)),
        out_shape=jax.ShapeDtypeStruct((shares, 16, LANES), jnp.float32),
        in_specs=[vmem] * (6 + len(others)) + [smem] * len(others),
        out_specs=vmem,
        scratch_shapes=[pltpu.VMEM((words, rows), jnp.int32) for _ in others],
        compiler_params=pltpu.CompilerParams(vmem_limit_bytes=8 << 20),
        name="gram",
    )(*held, *others, *starts)
    parts = lax.all_to_all(partial, "blk", 0, 0, tiled=True)
    factor, spread = pl.pallas_call(
        functools.partial(factor_kernel, vectors),
        out_shape=(
            jax.ShapeDtypeStruct((len(pairs), AGG_DEV), jnp.float32),
            jax.ShapeDtypeStruct((1, AGG_DEV), jnp.float32),
        ),
        in_specs=[vmem],
        out_specs=(vmem, vmem),
        compiler_params=pltpu.CompilerParams(vmem_limit_bytes=4 << 20),
        name="factor",
    )(parts)
    return factor, spread.reshape(AGG_DEV)


def solution(mesh):
    return jax.shard_map(
        shards,
        mesh=mesh,
        in_specs=(
            P(None, ("grp", "blk")),
            P(("grp", "blk")),
            P(None, ("grp", "blk")),
            P(None, ("grp", "blk")),
        ),
        out_specs=(P(None, ("grp", "blk")), P(("grp", "blk"))),
        check_vma=False,
    )
```

```python
import functools

import jax
import jax.numpy as jnp
from jax import lax
from jax.experimental import pallas as pl
from jax.experimental.pallas import tpu as pltpu
from jax.sharding import PartitionSpec as P

ROWS_DEV = 2048
AGG_DEV = 96
LANES = 128
NULL_MOST = 6.0
SPLIT = 11
SCALE_WHOLE = (2.0 ** (31 - SPLIT) - 1.0) / NULL_MOST
SCALE_SPLIT = (2.0 ** (2 * SPLIT - 1) - 1.0) / NULL_MOST
KEEP = (1 << SPLIT) - 1
PARITY_STEPS = 30


def pair_list(vectors):
    return [(p, q) for p in range(vectors) for q in range(p, vectors)]


def share_of(ids, shares):
    shift = 22
    factor = -(-(1 << shift) // AGG_DEV)
    most = shares * AGG_DEV - 1
    assert most * factor < 2**31 and (factor * AGG_DEV - (1 << shift)) * most < (1 << shift)
    return lax.shift_right_logical(ids * factor, shift)


def encode(table):
    words = 2 * table.shape[0] // 3
    whole = jnp.round(table[:words] * SCALE_WHOLE).astype(jnp.int32)
    split = jnp.round(table[words:] * SCALE_SPLIT).astype(jnp.int32)
    lower = [
        jnp.bitwise_and(split[r // 2 : r // 2 + 1] >> (0 if r % 2 else SPLIT), KEEP) for r in range(words)
    ]
    return jnp.bitwise_or(whole << SPLIT, jnp.concatenate(lower, axis=0))


def decode(words):
    values = [(word >> SPLIT).astype(jnp.float32) for word in words]
    for upper, lower in zip(words[0::2], words[1::2]):
        split = jnp.bitwise_or((upper << (32 - SPLIT)) >> (32 - 2 * SPLIT), jnp.bitwise_and(lower, KEEP))
        values.append(split.astype(jnp.float32))
    return values


def lane_pick(rows, low):
    return lax.gather(
        rows,
        low[:, :, None],
        lax.GatherDimensionNumbers(
            offset_dims=(),
            collapsed_slice_dims=(1,),
            start_index_map=(1,),
            operand_batching_dims=(0,),
            start_indices_batching_dims=(0,),
        ),
        slice_sizes=(1, 1),
        mode=lax.GatherScatterMode.PROMISE_IN_BOUNDS,
    )


def pick(picked, index, tables):
    low = jnp.bitwise_and(index, LANES - 1)
    for table_ref, base in tables:
        high = lax.shift_right_arithmetic(index - base, LANES.bit_length() - 1)
        for chunk in range(table_ref.shape[1] // LANES):
            found = high == chunk
            for word in range(len(picked)):
                row = table_ref[word : word + 1, chunk * LANES : (chunk + 1) * LANES]
                value = lane_pick(jnp.broadcast_to(row, index.shape), low)
                picked[word] = jnp.where(found, value, picked[word])
    return picked


def own_kernel(own_ref, index_ref, weight_hbm, ids_hbm, weight_ref, ids_ref, picked_ref, table_ref, sems):
    rows = own_ref.shape[1]
    moves = [
        pltpu.make_async_copy(weight_hbm, weight_ref, sems.at[0]),
        pltpu.make_async_copy(ids_hbm, ids_ref, sems.at[1]),
    ]
    for move in moves:
        move.start()
    table_ref[...] = encode(own_ref[...])
    for start in range(0, rows, LANES):
        here = slice(start, start + LANES)
        index = index_ref[:, here]
        zero = [jnp.zeros(index.shape, jnp.int32) for _ in range(table_ref.shape[0])]
        for word, value in enumerate(pick(zero, index, [(table_ref, rows)])):
            picked_ref[word, :, here] = value
    for move in moves:
        move.wait()


def to_wire(gram):
    tail = jnp.concatenate([gram[16:], jnp.zeros((8, LANES - AGG_DEV), gram.dtype)], axis=1)
    lanes = lax.broadcasted_iota(jnp.int32, (8, LANES), 1)
    rows = lax.broadcasted_iota(jnp.int32, (8, LANES), 0)
    out = []
    third = AGG_DEV // 3
    thirds = [pltpu.roll(tail, AGG_DEV - third * i, 1) for i in range(3)]
    for half in range(2):
        main = jnp.concatenate(
            [gram[8 * half : 8 * half + 8], jnp.zeros((8, LANES - AGG_DEV), gram.dtype)], axis=1
        )
        last = pltpu.roll(thirds[2], 5 - 3 * half, 0)
        side = jnp.where(rows < 5, thirds[half], last)
        out.append(jnp.where(lanes < AGG_DEV, main, side))
    return jnp.concatenate(out, axis=0)


def from_wire(wire):
    third = AGG_DEV // 3
    lanes = lax.broadcasted_iota(jnp.int32, (8, LANES), 1)
    rows = lax.broadcasted_iota(jnp.int32, (8, LANES), 0)
    first, second = wire[:8], wire[8:]
    last = jnp.where(rows < 3, pltpu.roll(first, 3, 0), pltpu.roll(second, 6, 0))
    thirds = [pltpu.roll(x, LANES - AGG_DEV + third * i, 1) for i, x in enumerate((first, second, last))]
    tail = jnp.where(lanes < third, thirds[0], jnp.where(lanes < 2 * third, thirds[1], thirds[2]))
    return jnp.concatenate([first, second, tail], axis=0)


def gram_kernel(shares, count, *refs):
    own_ref, index_ref, weight_ref, ids_ref, picked_ref = refs[:5]
    others, starts = refs[5 : 5 + count], refs[5 + count : 5 + 2 * count]
    out_ref, *table_refs = refs[5 + 2 * count :]
    vectors, rows = own_ref.shape
    pairs = pair_list(vectors)
    padded = 24
    tables = []
    for other_ref, start_ref, table_ref in zip(others, starts, table_refs):
        table_ref[...] = encode(other_ref[...])
        tables.append((table_ref, start_ref[0]))
    words = picked_ref.shape[0]
    scales = [1.0 / SCALE_WHOLE] * words + [1.0 / SCALE_SPLIT] * (vectors - words)
    half_shares = shares // 2
    gram = [jnp.zeros((half_shares * 2 * padded, AGG_DEV), jnp.float32) for _ in range(2)]
    step = LANES
    for first in range(0, rows, step):
        pieces = []
        for start in range(first, first + step, LANES):
            here = slice(start, start + LANES)
            weight = weight_ref[:, here]
            picked = pick([picked_ref[word, :, here] for word in range(words)], index_ref[:, here], tables)
            smooth = [
                own_ref[v : v + 1, here] - jnp.sum(weight * value, axis=0, keepdims=True) * scales[v]
                for v, value in enumerate(decode(picked))
            ]
            pieces.append([smooth[p] * smooth[q] for p, q in pairs])
        zero = jnp.zeros((padded - len(pairs), step), jnp.float32)
        terms = jnp.concatenate(
            [jnp.concatenate([half[i] for half in pieces], axis=1) for i in range(len(pairs))] + [zero],
            axis=0,
        )
        coarse = terms.astype(jnp.bfloat16).astype(jnp.float32)
        both = jnp.concatenate([coarse, terms - coarse], axis=0)
        share = share_of(ids_ref[:, first : first + step], shares)
        ids = ids_ref[:, first : first + step]
        within = ids - share * AGG_DEV
        columns = lax.broadcasted_iota(jnp.int32, (AGG_DEV, step), 0)
        one_hot = (columns == within).astype(jnp.float32).astype(jnp.bfloat16)
        for half in range(2):
            masked = jnp.concatenate(
                [jnp.where(share == half * half_shares + s, both, 0.0) for s in range(half_shares)], axis=0
            ).astype(jnp.bfloat16)
            gram[half] = gram[half] + lax.dot_general(
                masked,
                one_hot,
                (((1,), (1,)), ((), ())),
                preferred_element_type=jnp.float32,
            )
    for half in range(2):
        for s in range(half_shares):
            at = 2 * padded * s
            out_ref[half * half_shares + s] = to_wire(
                gram[half][at : at + padded] + gram[half][at + padded : at + 2 * padded]
            )


def factor_kernel(vectors, parts_ref, factor_ref, spread_ref):
    pairs = pair_list(vectors)
    total = parts_ref[0]
    for source in range(1, parts_ref.shape[0]):
        total = total + parts_ref[source]
    total = from_wire(total)[:, :AGG_DEV]
    entry = {}
    for i, (p, q) in enumerate(pairs):
        value = total[i : i + 1] * (AGG_DEV / ROWS_DEV)
        entry[p, q] = value + 1.0 if p == q else value
    upper = {}
    for j in range(vectors):
        pivot = entry[j, j]
        for k in range(j):
            pivot = pivot - upper[k, j] * upper[k, j]
        upper[j, j] = jnp.sqrt(pivot)
        for i in range(j + 1, vectors):
            rest = entry[j, i]
            for k in range(j):
                rest = rest - upper[k, i] * upper[k, j]
            upper[j, i] = rest / upper[j, j]
    for i, pair in enumerate(pairs):
        factor_ref[i : i + 1, :] = upper[pair]
    most = functools.reduce(jnp.maximum, [upper[j, j] for j in range(vectors)])
    least = functools.reduce(jnp.minimum, [upper[j, j] for j in range(vectors)])
    spread_ref[...] = jnp.log(most) - jnp.log(least)


def shards(nullspace, agg_ids, nbr_index, nbr_weight):
    vectors, rows = nullspace.shape
    assert vectors % 3 == 0 and rows % (2 * LANES) == 0
    words = 2 * vectors // 3
    groups, shares = lax.axis_size("grp"), lax.axis_size("blk")
    pairs = pair_list(vectors)
    assert len(pairs) == 21 and shares % 2 == 0
    vmem = pl.BlockSpec(memory_space=pltpu.VMEM)
    smem = pl.BlockSpec(memory_space=pltpu.SMEM)
    hbm = pl.BlockSpec(memory_space=pltpu.HBM)
    if groups == 2:
        others = [lax.ppermute(nullspace, "grp", [(0, 1), (1, 0)])]
        group = lax.axis_index("grp").astype(jnp.int32)
        for n in range(PARITY_STEPS):
            group = group * 3 + 2 * (n + 1)
        group = jnp.bitwise_and(group, 1)
        starts = [(2 * rows * (1 - group)).reshape(1)]
    else:
        others = [
            lax.ppermute(nullspace, "grp", [(i, i + 1) for i in range(groups - 1)]),
            lax.ppermute(nullspace, "grp", [(i + 1, i) for i in range(groups - 1)]),
        ]
        starts = [jnp.zeros((1,), jnp.int32), jnp.full((1,), 2 * rows, jnp.int32)]
    ids = agg_ids.reshape(1, rows)
    weight, ids, picked = pl.pallas_call(
        own_kernel,
        out_shape=[
            jax.ShapeDtypeStruct(nbr_weight.shape, nbr_weight.dtype),
            jax.ShapeDtypeStruct(ids.shape, ids.dtype),
            jax.ShapeDtypeStruct((words,) + nbr_index.shape, jnp.int32),
        ],
        in_specs=[vmem, vmem, hbm, hbm],
        out_specs=[vmem] * 3,
        scratch_shapes=[pltpu.VMEM((words, rows), jnp.int32), pltpu.SemaphoreType.DMA((2,))],
        compiler_params=pltpu.CompilerParams(vmem_limit_bytes=4 << 20),
        cost_estimate=pl.CostEstimate(flops=1 << 22, bytes_accessed=1 << 18, transcendentals=0),
        name="own",
    )(
        nullspace,
        nbr_index,
        pltpu.with_memory_space_constraint(nbr_weight, pltpu.HBM),
        pltpu.with_memory_space_constraint(ids, pltpu.HBM),
    )
    partial = pl.pallas_call(
        functools.partial(gram_kernel, shares, len(others)),
        out_shape=jax.ShapeDtypeStruct((shares, 16, LANES), jnp.float32),
        in_specs=[vmem] * (5 + len(others)) + [smem] * len(others),
        out_specs=vmem,
        scratch_shapes=[pltpu.VMEM((words, rows), jnp.int32) for _ in others],
        compiler_params=pltpu.CompilerParams(vmem_limit_bytes=8 << 20),
        name="gram",
    )(nullspace, nbr_index, weight, ids, picked, *others, *starts)
    parts = lax.all_to_all(partial, "blk", 0, 0, tiled=True)
    factor, spread = pl.pallas_call(
        functools.partial(factor_kernel, vectors),
        out_shape=(
            jax.ShapeDtypeStruct((len(pairs), AGG_DEV), jnp.float32),
            jax.ShapeDtypeStruct((1, AGG_DEV), jnp.float32),
        ),
        in_specs=[vmem],
        out_specs=(vmem, vmem),
        compiler_params=pltpu.CompilerParams(vmem_limit_bytes=4 << 20),
        name="factor",
    )(parts)
    return factor, spread.reshape(AGG_DEV)


def solution(mesh):
    return jax.shard_map(
        shards,
        mesh=mesh,
        in_specs=(
            P(None, ("grp", "blk")),
            P(("grp", "blk")),
            P(None, ("grp", "blk")),
            P(None, ("grp", "blk")),
        ),
        out_specs=(P(None, ("grp", "blk")), P(("grp", "blk"))),
        check_vma=False,
    )
```

```python
import functools

import jax
import jax.numpy as jnp
from jax import lax
from jax.experimental import pallas as pl
from jax.experimental.pallas import tpu as pltpu
from jax.sharding import PartitionSpec as P

ROWS_DEV = 2048
AGG_DEV = 96
LANES = 128
NULL_MOST = 6.0
SPLIT = 11
SCALE_WHOLE = (2.0 ** (31 - SPLIT) - 1.0) / NULL_MOST
SCALE_SPLIT = (2.0 ** (2 * SPLIT - 1) - 1.0) / NULL_MOST
KEEP = (1 << SPLIT) - 1
PARITY_STEPS = 30


def pair_list(vectors):
    return [(p, q) for p in range(vectors) for q in range(p, vectors)]


def share_of(ids, shares):
    shift = 22
    factor = -(-(1 << shift) // AGG_DEV)
    most = shares * AGG_DEV - 1
    assert most * factor < 2**31 and (factor * AGG_DEV - (1 << shift)) * most < (1 << shift)
    return lax.shift_right_logical(ids * factor, shift)


def encode(table):
    words = 2 * table.shape[0] // 3
    whole = jnp.round(table[:words] * SCALE_WHOLE).astype(jnp.int32)
    split = jnp.round(table[words:] * SCALE_SPLIT).astype(jnp.int32)
    lower = [
        jnp.bitwise_and(split[r // 2 : r // 2 + 1] >> (0 if r % 2 else SPLIT), KEEP) for r in range(words)
    ]
    return jnp.bitwise_or(whole << SPLIT, jnp.concatenate(lower, axis=0))


def decode(words):
    values = [(word >> SPLIT).astype(jnp.float32) for word in words]
    for upper, lower in zip(words[0::2], words[1::2]):
        split = jnp.bitwise_or((upper << (32 - SPLIT)) >> (32 - 2 * SPLIT), jnp.bitwise_and(lower, KEEP))
        values.append(split.astype(jnp.float32))
    return values


def lane_pick(rows, low):
    return lax.gather(
        rows,
        low[:, :, None],
        lax.GatherDimensionNumbers(
            offset_dims=(),
            collapsed_slice_dims=(1,),
            start_index_map=(1,),
            operand_batching_dims=(0,),
            start_indices_batching_dims=(0,),
        ),
        slice_sizes=(1, 1),
        mode=lax.GatherScatterMode.PROMISE_IN_BOUNDS,
    )


def pick(picked, index, tables, first=0):
    low = jnp.bitwise_and(index, LANES - 1)
    for table_ref, base in tables:
        high = lax.shift_right_arithmetic(index - base, LANES.bit_length() - 1)
        for chunk in range(table_ref.shape[1] // LANES):
            found = high == chunk
            for word in range(len(picked)):
                row = table_ref[first + word : first + word + 1, chunk * LANES : (chunk + 1) * LANES]
                value = lane_pick(jnp.broadcast_to(row, index.shape), low)
                picked[word] = jnp.where(found, value, picked[word])
    return picked


def own_kernel(own_ref, index_ref, weight_hbm, ids_hbm, weight_ref, ids_ref, picked_ref, table_ref, sems):
    rows = own_ref.shape[1]
    moves = [
        pltpu.make_async_copy(weight_hbm, weight_ref, sems.at[0]),
        pltpu.make_async_copy(ids_hbm, ids_ref, sems.at[1]),
    ]
    for move in moves:
        move.start()
    table_ref[...] = encode(own_ref[...])
    for start in range(0, rows, LANES):
        here = slice(start, start + LANES)
        index = index_ref[:, here]
        for word in range(0, table_ref.shape[0], 2):
            zero = [jnp.zeros(index.shape, jnp.int32) for _ in range(2)]
            found = pick(zero, index, [(table_ref, rows)], word)
            for i, value in enumerate(found):
                picked_ref[word + i, :, here] = value
    for move in moves:
        move.wait()


def to_wire(gram):
    tail = jnp.concatenate([gram[16:], jnp.zeros((8, LANES - AGG_DEV), gram.dtype)], axis=1)
    lanes = lax.broadcasted_iota(jnp.int32, (8, LANES), 1)
    rows = lax.broadcasted_iota(jnp.int32, (8, LANES), 0)
    out = []
    third = AGG_DEV // 3
    thirds = [pltpu.roll(tail, AGG_DEV - third * i, 1) for i in range(3)]
    for half in range(2):
        main = jnp.concatenate(
            [gram[8 * half : 8 * half + 8], jnp.zeros((8, LANES - AGG_DEV), gram.dtype)], axis=1
        )
        last = pltpu.roll(thirds[2], 5 - 3 * half, 0)
        side = jnp.where(rows < 5, thirds[half], last)
        out.append(jnp.where(lanes < AGG_DEV, main, side))
    return jnp.concatenate(out, axis=0)


def from_wire(wire):
    third = AGG_DEV // 3
    lanes = lax.broadcasted_iota(jnp.int32, (8, LANES), 1)
    rows = lax.broadcasted_iota(jnp.int32, (8, LANES), 0)
    first, second = wire[:8], wire[8:]
    last = jnp.where(rows < 3, pltpu.roll(first, 3, 0), pltpu.roll(second, 6, 0))
    thirds = [pltpu.roll(x, LANES - AGG_DEV + third * i, 1) for i, x in enumerate((first, second, last))]
    tail = jnp.where(lanes < third, thirds[0], jnp.where(lanes < 2 * third, thirds[1], thirds[2]))
    return jnp.concatenate([first, second, tail], axis=0)


def fold(values, row):
    values = list(values) + [None] * (8 - len(values))
    for half in (4, 2, 1):
        upper = jnp.bitwise_and(row, half) != 0
        values = [fold_two(one, two, half, upper) for one, two in zip(values[0::2], values[1::2])]
    return values[0]


def fold_two(one, two, half, upper):
    if one is None:
        return None
    if two is None:
        return one + across(one, half, upper)
    return jnp.where(upper, two, one) + across(jnp.where(upper, one, two), half, upper)


def across(x, half, upper):
    if half == 4:
        return pltpu.roll(x, 4, 0)
    return jnp.where(upper, pltpu.roll(x, half, 0), pltpu.roll(x, 8 - half, 0))


def shuffle(x, index):
    return lax.gather(
        x,
        index[:, :, None],
        lax.GatherDimensionNumbers(
            offset_dims=(),
            collapsed_slice_dims=(0,),
            start_index_map=(0,),
            operand_batching_dims=(1,),
            start_indices_batching_dims=(1,),
        ),
        slice_sizes=(1, 1),
        mode=lax.GatherScatterMode.PROMISE_IN_BOUNDS,
    )


def rows_of(wanted, row):
    out = jnp.zeros(row.shape, jnp.int32)
    for s, value in enumerate(wanted):
        out = jnp.where(row == s, value, out)
    return out


def gram_kernel(shares, count, *refs):
    own_ref, index_ref, weight_ref, ids_ref, picked_ref = refs[:5]
    others, starts = refs[5 : 5 + count], refs[5 + count : 5 + 2 * count]
    out_ref, *table_refs = refs[5 + 2 * count :]
    vectors, rows = own_ref.shape
    pairs = pair_list(vectors)
    padded = 24
    tables = []
    for other_ref, start_ref, table_ref in zip(others, starts, table_refs):
        table_ref[...] = encode(other_ref[...])
        tables.append((table_ref, start_ref[0]))
    words = picked_ref.shape[0]
    scales = [1.0 / SCALE_WHOLE] * words + [1.0 / SCALE_SPLIT] * (vectors - words)
    half_shares = shares // 2
    gram = [jnp.zeros((half_shares * 2 * padded, AGG_DEV), jnp.float32) for _ in range(4)]
    step = LANES
    rows8 = lax.broadcasted_iota(jnp.int32, (8, LANES), 0)
    place = [4 * (v & 1) + (v & 2) + (v >> 2) for v in range(8)]
    order = rows_of([place.index(s) for s in range(8)], rows8)
    listed = pairs + [(0, 0)] * (padded - len(pairs))
    sides = [
        tuple(rows_of([place[pair[side]] for pair in listed[at : at + 8]], rows8) for side in range(2))
        for at in range(0, padded, 8)
    ]
    for first in range(0, rows, step):
        here = slice(first, first + step)
        picked = pick([picked_ref[word, :, here] for word in range(words)], index_ref[:, here], tables)
        values = [value * scale for value, scale in zip(decode(picked), scales)]
        near = fold([weight_ref[:, here] * value for value in values], rows8)
        own = jnp.concatenate([own_ref[:, here], jnp.zeros((8 - vectors, step), jnp.float32)], axis=0)
        smooth = shuffle(own, order) - near
        terms = jnp.concatenate([shuffle(smooth, p) * shuffle(smooth, q) for p, q in sides], axis=0)
        coarse = terms.astype(jnp.bfloat16).astype(jnp.float32)
        both = jnp.concatenate([coarse, terms - coarse], axis=0)
        share = jnp.broadcast_to(share_of(ids_ref[:, first : first + step], shares), (2 * padded, step))
        ids = ids_ref[:, first : first + step]
        within = ids - share[:1] * AGG_DEV
        columns = lax.broadcasted_iota(jnp.int32, (AGG_DEV, step), 0)
        one_hot = (columns == within).astype(jnp.float32).astype(jnp.bfloat16)
        for half in range(2):
            masked = jnp.concatenate(
                [jnp.where(share == half * half_shares + s, both, 0.0) for s in range(half_shares)], axis=0
            ).astype(jnp.bfloat16)
            turn = 2 * (first // step % 2) + half
            gram[turn] = gram[turn] + lax.dot_general(
                masked,
                one_hot,
                (((1,), (1,)), ((), ())),
                preferred_element_type=jnp.float32,
            )
    gram = [gram[half] + gram[2 + half] for half in range(2)]
    for half in range(2):
        for s in range(half_shares):
            at = 2 * padded * s
            out_ref[half * half_shares + s] = to_wire(
                gram[half][at : at + padded] + gram[half][at + padded : at + 2 * padded]
            )


def factor_kernel(vectors, parts_ref, factor_ref, spread_ref):
    pairs = pair_list(vectors)
    sums = [parts_ref[source] for source in range(parts_ref.shape[0])]
    while len(sums) > 1:
        odd = sums[len(sums) // 2 * 2 :]
        sums = [one + two for one, two in zip(sums[0::2], sums[1::2])] + odd
    total = from_wire(sums[0])[:, :AGG_DEV]
    entry = {}
    for i, (p, q) in enumerate(pairs):
        value = total[i : i + 1] * (AGG_DEV / ROWS_DEV)
        entry[p, q] = value + 1.0 if p == q else value
    upper = {}
    for j in range(vectors):
        pivot = entry[j, j]
        for k in range(j):
            pivot = pivot - upper[k, j] * upper[k, j]
        upper[j, j] = jnp.sqrt(pivot)
        for i in range(j + 1, vectors):
            rest = entry[j, i]
            for k in range(j):
                rest = rest - upper[k, i] * upper[k, j]
            upper[j, i] = rest / upper[j, j]
    for i, pair in enumerate(pairs):
        factor_ref[i : i + 1, :] = upper[pair]
    most = functools.reduce(jnp.maximum, [upper[j, j] for j in range(vectors)])
    least = functools.reduce(jnp.minimum, [upper[j, j] for j in range(vectors)])
    spread_ref[...] = jnp.log(most) - jnp.log(least)


def shards(nullspace, agg_ids, nbr_index, nbr_weight):
    vectors, rows = nullspace.shape
    assert vectors % 3 == 0 and rows % (2 * LANES) == 0
    words = 2 * vectors // 3
    groups, shares = lax.axis_size("grp"), lax.axis_size("blk")
    pairs = pair_list(vectors)
    assert len(pairs) == 21 and shares % 2 == 0
    vmem = pl.BlockSpec(memory_space=pltpu.VMEM)
    smem = pl.BlockSpec(memory_space=pltpu.SMEM)
    hbm = pl.BlockSpec(memory_space=pltpu.HBM)
    if groups == 2:
        others = [lax.ppermute(nullspace, "grp", [(0, 1), (1, 0)])]
        group = lax.axis_index("grp").astype(jnp.int32)
        for n in range(PARITY_STEPS):
            group = group * 3 + 2 * (n + 1)
        group = jnp.bitwise_and(group, 1)
        starts = [(2 * rows * (1 - group)).reshape(1)]
    else:
        others = [
            lax.ppermute(nullspace, "grp", [(i, i + 1) for i in range(groups - 1)]),
            lax.ppermute(nullspace, "grp", [(i + 1, i) for i in range(groups - 1)]),
        ]
        starts = [jnp.zeros((1,), jnp.int32), jnp.full((1,), 2 * rows, jnp.int32)]
    ids = agg_ids.reshape(1, rows)
    weight, ids, picked = pl.pallas_call(
        own_kernel,
        out_shape=[
            jax.ShapeDtypeStruct(nbr_weight.shape, nbr_weight.dtype),
            jax.ShapeDtypeStruct(ids.shape, ids.dtype),
            jax.ShapeDtypeStruct((words,) + nbr_index.shape, jnp.int32),
        ],
        in_specs=[vmem, vmem, hbm, hbm],
        out_specs=[vmem] * 3,
        scratch_shapes=[pltpu.VMEM((words, rows), jnp.int32), pltpu.SemaphoreType.DMA((2,))],
        compiler_params=pltpu.CompilerParams(vmem_limit_bytes=4 << 20),
        cost_estimate=pl.CostEstimate(flops=1 << 22, bytes_accessed=1 << 18, transcendentals=0),
        name="own",
    )(
        nullspace,
        nbr_index,
        pltpu.with_memory_space_constraint(nbr_weight, pltpu.HBM),
        pltpu.with_memory_space_constraint(ids, pltpu.HBM),
    )
    partial = pl.pallas_call(
        functools.partial(gram_kernel, shares, len(others)),
        out_shape=jax.ShapeDtypeStruct((shares, 16, LANES), jnp.float32),
        in_specs=[vmem] * (5 + len(others)) + [smem] * len(others),
        out_specs=vmem,
        scratch_shapes=[pltpu.VMEM((words, rows), jnp.int32) for _ in others],
        compiler_params=pltpu.CompilerParams(vmem_limit_bytes=8 << 20),
        name="gram",
    )(nullspace, nbr_index, weight, ids, picked, *others, *starts)
    parts = lax.all_to_all(partial, "blk", 0, 0, tiled=True)
    factor, spread = pl.pallas_call(
        functools.partial(factor_kernel, vectors),
        out_shape=(
            jax.ShapeDtypeStruct((len(pairs), AGG_DEV), jnp.float32),
            jax.ShapeDtypeStruct((1, AGG_DEV), jnp.float32),
        ),
        in_specs=[vmem],
        out_specs=(vmem, vmem),
        compiler_params=pltpu.CompilerParams(vmem_limit_bytes=4 << 20),
        name="factor",
    )(parts)
    return factor, spread.reshape(AGG_DEV)


def solution(mesh):
    return jax.shard_map(
        shards,
        mesh=mesh,
        in_specs=(
            P(None, ("grp", "blk")),
            P(("grp", "blk")),
            P(None, ("grp", "blk")),
            P(None, ("grp", "blk")),
        ),
        out_specs=(P(None, ("grp", "blk")), P(("grp", "blk"))),
        check_vma=False,
    )
```

```python
import functools

import jax
import jax.numpy as jnp
from jax import lax
from jax.experimental import pallas as pl
from jax.experimental.pallas import tpu as pltpu
from jax.sharding import PartitionSpec as P

ROWS_DEV = 2048
AGG_DEV = 96
LANES = 128
NULL_MOST = 6.0
SPLIT = 11
SCALE_WHOLE = (2.0 ** (31 - SPLIT) - 1.0) / NULL_MOST
SCALE_SPLIT = (2.0 ** (2 * SPLIT - 1) - 1.0) / NULL_MOST
KEEP = (1 << SPLIT) - 1
PARITY_STEPS = 30


def pair_list(vectors):
    return [(p, q) for p in range(vectors) for q in range(p, vectors)]


def share_of(ids, shares):
    shift = 22
    factor = -(-(1 << shift) // AGG_DEV)
    most = shares * AGG_DEV - 1
    assert most * factor < 2**31 and (factor * AGG_DEV - (1 << shift)) * most < (1 << shift)
    return lax.shift_right_logical(ids * factor, shift)


def encode(table):
    words = 2 * table.shape[0] // 3
    whole = jnp.round(table[:words] * SCALE_WHOLE).astype(jnp.int32)
    split = jnp.round(table[words:] * SCALE_SPLIT).astype(jnp.int32)
    lower = [
        jnp.bitwise_and(split[r // 2 : r // 2 + 1] >> (0 if r % 2 else SPLIT), KEEP) for r in range(words)
    ]
    return jnp.bitwise_or(whole << SPLIT, jnp.concatenate(lower, axis=0))


def decode(words):
    values = [(word >> SPLIT).astype(jnp.float32) for word in words]
    for upper, lower in zip(words[0::2], words[1::2]):
        split = jnp.bitwise_or((upper << (32 - SPLIT)) >> (32 - 2 * SPLIT), jnp.bitwise_and(lower, KEEP))
        values.append(split.astype(jnp.float32))
    return values


def lane_pick(rows, low):
    return lax.gather(
        rows,
        low[:, :, None],
        lax.GatherDimensionNumbers(
            offset_dims=(),
            collapsed_slice_dims=(1,),
            start_index_map=(1,),
            operand_batching_dims=(0,),
            start_indices_batching_dims=(0,),
        ),
        slice_sizes=(1, 1),
        mode=lax.GatherScatterMode.PROMISE_IN_BOUNDS,
    )


def pick(picked, index, tables, first=0):
    low = jnp.bitwise_and(index, LANES - 1)
    for table_ref, base in tables:
        high = lax.shift_right_arithmetic(index - base, LANES.bit_length() - 1)
        for chunk in range(table_ref.shape[1] // LANES):
            found = high == chunk
            for word in range(len(picked)):
                row = table_ref[first + word : first + word + 1, chunk * LANES : (chunk + 1) * LANES]
                value = lane_pick(jnp.broadcast_to(row, index.shape), low)
                picked[word] = jnp.where(found, value, picked[word])
    return picked


def own_kernel(own_ref, index_ref, picked_ref, table_ref):
    rows = own_ref.shape[1]
    table_ref[...] = encode(own_ref[...])
    for start in range(0, rows, LANES):
        here = slice(start, start + LANES)
        index = index_ref[:, here]
        for word in range(0, table_ref.shape[0], 2):
            zero = [jnp.zeros(index.shape, jnp.int32) for _ in range(2)]
            found = pick(zero, index, [(table_ref, rows)], word)
            for i, value in enumerate(found):
                picked_ref[word + i, :, here] = value


def to_wire(gram):
    tail = jnp.concatenate([gram[16:], jnp.zeros((8, LANES - AGG_DEV), gram.dtype)], axis=1)
    lanes = lax.broadcasted_iota(jnp.int32, (8, LANES), 1)
    rows = lax.broadcasted_iota(jnp.int32, (8, LANES), 0)
    out = []
    third = AGG_DEV // 3
    thirds = [pltpu.roll(tail, AGG_DEV - third * i, 1) for i in range(3)]
    for half in range(2):
        main = jnp.concatenate(
            [gram[8 * half : 8 * half + 8], jnp.zeros((8, LANES - AGG_DEV), gram.dtype)], axis=1
        )
        last = pltpu.roll(thirds[2], 5 - 3 * half, 0)
        side = jnp.where(rows < 5, thirds[half], last)
        out.append(jnp.where(lanes < AGG_DEV, main, side))
    return jnp.concatenate(out, axis=0)


def from_wire(wire):
    third = AGG_DEV // 3
    lanes = lax.broadcasted_iota(jnp.int32, (8, LANES), 1)
    rows = lax.broadcasted_iota(jnp.int32, (8, LANES), 0)
    first, second = wire[:8], wire[8:]
    last = jnp.where(rows < 3, pltpu.roll(first, 3, 0), pltpu.roll(second, 6, 0))
    thirds = [pltpu.roll(x, LANES - AGG_DEV + third * i, 1) for i, x in enumerate((first, second, last))]
    tail = jnp.where(lanes < third, thirds[0], jnp.where(lanes < 2 * third, thirds[1], thirds[2]))
    return jnp.concatenate([first, second, tail], axis=0)


def fold(values, row):
    values = list(values) + [None] * (8 - len(values))
    for half in (4, 2, 1):
        upper = jnp.bitwise_and(row, half) != 0
        values = [fold_two(one, two, half, upper) for one, two in zip(values[0::2], values[1::2])]
    return values[0]


def fold_two(one, two, half, upper):
    if one is None:
        return None
    if two is None:
        return one + across(one, half, upper)
    return jnp.where(upper, two, one) + across(jnp.where(upper, one, two), half, upper)


def across(x, half, upper):
    if half == 4:
        return pltpu.roll(x, 4, 0)
    return jnp.where(upper, pltpu.roll(x, half, 0), pltpu.roll(x, 8 - half, 0))


def shuffle(x, index):
    return lax.gather(
        x,
        index[:, :, None],
        lax.GatherDimensionNumbers(
            offset_dims=(),
            collapsed_slice_dims=(0,),
            start_index_map=(0,),
            operand_batching_dims=(1,),
            start_indices_batching_dims=(1,),
        ),
        slice_sizes=(1, 1),
        mode=lax.GatherScatterMode.PROMISE_IN_BOUNDS,
    )


def rows_of(wanted, row):
    out = jnp.zeros(row.shape, jnp.int32)
    for s, value in enumerate(wanted):
        out = jnp.where(row == s, value, out)
    return out


def gram_kernel(shares, count, *refs):
    own_ref, index_ref, weight_ref, ids_ref, picked_ref = refs[:5]
    others, starts = refs[5 : 5 + count], refs[5 + count : 5 + 2 * count]
    out_ref, *table_refs = refs[5 + 2 * count :]
    vectors, rows = own_ref.shape
    pairs = pair_list(vectors)
    padded = 24
    tables = []
    for other_ref, start_ref, table_ref in zip(others, starts, table_refs):
        table_ref[...] = encode(other_ref[...])
        tables.append((table_ref, start_ref[0]))
    words = picked_ref.shape[0]
    half_shares = shares // 2
    gram = [jnp.zeros((half_shares * 2 * padded, AGG_DEV), jnp.float32) for _ in range(4)]
    step = LANES
    rows8 = lax.broadcasted_iota(jnp.int32, (8, LANES), 0)
    place = [4 * (v & 1) + (v & 2) + (v >> 2) for v in range(8)]
    unit = jnp.where(rows_of(place, rows8) < words, 1.0 / SCALE_WHOLE, 1.0 / SCALE_SPLIT)
    order = rows_of([place.index(s) for s in range(8)], rows8)
    listed = pairs + [(0, 0)] * (padded - len(pairs))
    sides = [
        tuple(rows_of([place[pair[side]] for pair in listed[at : at + 8]], rows8) for side in range(2))
        for at in range(0, padded, 8)
    ]
    for first in range(0, rows, step):
        here = slice(first, first + step)
        picked = pick([picked_ref[word, :, here] for word in range(words)], index_ref[:, here], tables)
        near = fold([weight_ref[:, here] * value for value in decode(picked)], rows8) * unit
        own = jnp.concatenate([own_ref[:, here], jnp.zeros((8 - vectors, step), jnp.float32)], axis=0)
        smooth = shuffle(own, order) - near
        terms = jnp.concatenate([shuffle(smooth, p) * shuffle(smooth, q) for p, q in sides], axis=0)
        coarse = terms.astype(jnp.bfloat16).astype(jnp.float32)
        both = jnp.concatenate([coarse, terms - coarse], axis=0)
        share = jnp.broadcast_to(share_of(ids_ref[:, first : first + step], shares), (2 * padded, step))
        ids = ids_ref[:, first : first + step]
        within = ids - share[:1] * AGG_DEV
        columns = lax.broadcasted_iota(jnp.int32, (AGG_DEV, step), 0)
        one_hot = (columns == within).astype(jnp.float32).astype(jnp.bfloat16)
        for half in range(2):
            masked = jnp.concatenate(
                [jnp.where(share == half * half_shares + s, both, 0.0) for s in range(half_shares)], axis=0
            ).astype(jnp.bfloat16)
            turn = 2 * (first // step % 2) + half
            gram[turn] = gram[turn] + lax.dot_general(
                masked,
                one_hot,
                (((1,), (1,)), ((), ())),
                preferred_element_type=jnp.float32,
            )
    gram = [gram[half] + gram[2 + half] for half in range(2)]
    for half in range(2):
        for s in range(half_shares):
            at = 2 * padded * s
            out_ref[half * half_shares + s] = to_wire(
                gram[half][at : at + padded] + gram[half][at + padded : at + 2 * padded]
            )


def factor_kernel(vectors, parts_ref, factor_ref, spread_ref):
    pairs = pair_list(vectors)
    sums = [parts_ref[source] for source in range(parts_ref.shape[0])]
    while len(sums) > 1:
        odd = sums[len(sums) // 2 * 2 :]
        sums = [one + two for one, two in zip(sums[0::2], sums[1::2])] + odd
    total = from_wire(sums[0])[:, :AGG_DEV]
    entry = {}
    for i, (p, q) in enumerate(pairs):
        value = total[i : i + 1] * (AGG_DEV / ROWS_DEV)
        entry[p, q] = value + 1.0 if p == q else value
    upper = {}
    for j in range(vectors):
        pivot = entry[j, j]
        for k in range(j):
            pivot = pivot - upper[k, j] * upper[k, j]
        upper[j, j] = jnp.sqrt(pivot)
        for i in range(j + 1, vectors):
            rest = entry[j, i]
            for k in range(j):
                rest = rest - upper[k, i] * upper[k, j]
            upper[j, i] = rest / upper[j, j]
    for i, pair in enumerate(pairs):
        factor_ref[i : i + 1, :] = upper[pair]
    most = functools.reduce(jnp.maximum, [upper[j, j] for j in range(vectors)])
    least = functools.reduce(jnp.minimum, [upper[j, j] for j in range(vectors)])
    spread_ref[...] = jnp.log(most) - jnp.log(least)


def shards(nullspace, agg_ids, nbr_index, nbr_weight):
    vectors, rows = nullspace.shape
    assert vectors % 3 == 0 and rows % (2 * LANES) == 0
    words = 2 * vectors // 3
    groups, shares = lax.axis_size("grp"), lax.axis_size("blk")
    pairs = pair_list(vectors)
    assert len(pairs) == 21 and shares % 2 == 0
    vmem = pl.BlockSpec(memory_space=pltpu.VMEM)
    smem = pl.BlockSpec(memory_space=pltpu.SMEM)
    if groups == 2:
        others = [lax.ppermute(nullspace, "grp", [(0, 1), (1, 0)])]
        group = jnp.bitwise_xor(lax.axis_index("grp").astype(jnp.int32), 6) * 3
        for n in range(PARITY_STEPS):
            group = group * 3 + 2 * (n + 1)
        group = jnp.bitwise_and(group, 1)
        starts = [(2 * rows * (1 - group)).reshape(1)]
    else:
        others = [
            lax.ppermute(nullspace, "grp", [(i, i + 1) for i in range(groups - 1)]),
            lax.ppermute(nullspace, "grp", [(i + 1, i) for i in range(groups - 1)]),
        ]
        starts = [jnp.zeros((1,), jnp.int32), jnp.full((1,), 2 * rows, jnp.int32)]
    ids = agg_ids.reshape(1, rows)
    picked = pl.pallas_call(
        own_kernel,
        out_shape=jax.ShapeDtypeStruct((words,) + nbr_index.shape, jnp.int32),
        in_specs=[vmem, vmem],
        out_specs=vmem,
        scratch_shapes=[pltpu.VMEM((words, rows), jnp.int32)],
        compiler_params=pltpu.CompilerParams(vmem_limit_bytes=4 << 20),
        cost_estimate=pl.CostEstimate(flops=1 << 22, bytes_accessed=1 << 18, transcendentals=0),
        name="own",
    )(nullspace, nbr_index)
    partial = pl.pallas_call(
        functools.partial(gram_kernel, shares, len(others)),
        out_shape=jax.ShapeDtypeStruct((shares, 16, LANES), jnp.float32),
        in_specs=[vmem] * (5 + len(others)) + [smem] * len(others),
        out_specs=vmem,
        scratch_shapes=[pltpu.VMEM((words, rows), jnp.int32) for _ in others],
        compiler_params=pltpu.CompilerParams(vmem_limit_bytes=8 << 20),
        name="gram",
    )(nullspace, nbr_index, nbr_weight, ids, picked, *others, *starts)
    parts = lax.all_to_all(partial, "blk", 0, 0, tiled=True)
    factor, spread = pl.pallas_call(
        functools.partial(factor_kernel, vectors),
        out_shape=(
            jax.ShapeDtypeStruct((len(pairs), AGG_DEV), jnp.float32),
            jax.ShapeDtypeStruct((1, AGG_DEV), jnp.float32),
        ),
        in_specs=[vmem],
        out_specs=(vmem, vmem),
        compiler_params=pltpu.CompilerParams(vmem_limit_bytes=4 << 20),
        name="factor",
    )(parts)
    return factor, spread.reshape(AGG_DEV)


def solution(mesh):
    return jax.shard_map(
        shards,
        mesh=mesh,
        in_specs=(
            P(None, ("grp", "blk")),
            P(("grp", "blk")),
            P(None, ("grp", "blk")),
            P(None, ("grp", "blk")),
        ),
        out_specs=(P(None, ("grp", "blk")), P(("grp", "blk"))),
        check_vma=False,
    )
```

```python
import functools

import jax
import jax.numpy as jnp
from jax import lax
from jax.experimental import pallas as pl
from jax.experimental.pallas import tpu as pltpu
from jax.sharding import PartitionSpec as P

ROWS_DEV = 2048
AGG_DEV = 96
LANES = 128
NULL_MOST = 6.0
SPLIT = 11
SCALE_WHOLE = (2.0 ** (31 - SPLIT) - 1.0) / NULL_MOST
SCALE_SPLIT = (2.0 ** (2 * SPLIT - 1) - 1.0) / NULL_MOST
KEEP = (1 << SPLIT) - 1
PARITY_STEPS = 30


def pair_list(vectors):
    return [(p, q) for p in range(vectors) for q in range(p, vectors)]


def share_of(ids, shares):
    shift = 22
    factor = -(-(1 << shift) // AGG_DEV)
    most = shares * AGG_DEV - 1
    assert most * factor < 2**31 and (factor * AGG_DEV - (1 << shift)) * most < (1 << shift)
    return lax.shift_right_logical(ids * factor, shift)


def encode(table):
    words = 2 * table.shape[0] // 3
    whole = jnp.round(table[:words] * SCALE_WHOLE).astype(jnp.int32)
    split = jnp.round(table[words:] * SCALE_SPLIT).astype(jnp.int32)
    lower = [
        jnp.bitwise_and(split[r // 2 : r // 2 + 1] >> (0 if r % 2 else SPLIT), KEEP) for r in range(words)
    ]
    return jnp.bitwise_or(whole << SPLIT, jnp.concatenate(lower, axis=0))


def decode(words):
    values = [(word >> SPLIT).astype(jnp.float32) for word in words]
    for upper, lower in zip(words[0::2], words[1::2]):
        split = jnp.bitwise_or((upper << (32 - SPLIT)) >> (32 - 2 * SPLIT), jnp.bitwise_and(lower, KEEP))
        values.append(split.astype(jnp.float32))
    return values


def lane_pick(rows, low):
    return lax.gather(
        rows,
        low[:, :, None],
        lax.GatherDimensionNumbers(
            offset_dims=(),
            collapsed_slice_dims=(1,),
            start_index_map=(1,),
            operand_batching_dims=(0,),
            start_indices_batching_dims=(0,),
        ),
        slice_sizes=(1, 1),
        mode=lax.GatherScatterMode.PROMISE_IN_BOUNDS,
    )


def pick(picked, index, tables, first=0):
    low = jnp.bitwise_and(index, LANES - 1)
    for table_ref, base in tables:
        high = lax.shift_right_arithmetic(index - base, LANES.bit_length() - 1)
        for chunk in range(table_ref.shape[1] // LANES):
            found = high == chunk
            for word in range(len(picked)):
                row = table_ref[first + word : first + word + 1, chunk * LANES : (chunk + 1) * LANES]
                value = lane_pick(jnp.broadcast_to(row, index.shape), low)
                picked[word] = jnp.where(found, value, picked[word])
    return picked


def own_kernel(own_ref, index_ref, picked_ref, table_ref):
    rows = own_ref.shape[1]
    table_ref[...] = encode(own_ref[...])
    for start in range(0, rows, LANES):
        here = slice(start, start + LANES)
        index = index_ref[:, here]
        for word in range(0, table_ref.shape[0], 2):
            zero = [jnp.zeros(index.shape, jnp.int32) for _ in range(2)]
            found = pick(zero, index, [(table_ref, rows)], word)
            for i, value in enumerate(found):
                picked_ref[word + i, :, here] = value


def to_wire(gram):
    tail = jnp.concatenate([gram[16:], jnp.zeros((8, LANES - AGG_DEV), gram.dtype)], axis=1)
    lanes = lax.broadcasted_iota(jnp.int32, (8, LANES), 1)
    rows = lax.broadcasted_iota(jnp.int32, (8, LANES), 0)
    out = []
    third = AGG_DEV // 3
    thirds = [pltpu.roll(tail, AGG_DEV - third * i, 1) for i in range(3)]
    for half in range(2):
        main = jnp.concatenate(
            [gram[8 * half : 8 * half + 8], jnp.zeros((8, LANES - AGG_DEV), gram.dtype)], axis=1
        )
        last = pltpu.roll(thirds[2], 5 - 3 * half, 0)
        side = jnp.where(rows < 5, thirds[half], last)
        out.append(jnp.where(lanes < AGG_DEV, main, side))
    return jnp.concatenate(out, axis=0)


def from_wire(wire):
    third = AGG_DEV // 3
    lanes = lax.broadcasted_iota(jnp.int32, (8, LANES), 1)
    rows = lax.broadcasted_iota(jnp.int32, (8, LANES), 0)
    first, second = wire[:8], wire[8:]
    last = jnp.where(rows < 3, pltpu.roll(first, 3, 0), pltpu.roll(second, 6, 0))
    thirds = [pltpu.roll(x, LANES - AGG_DEV + third * i, 1) for i, x in enumerate((first, second, last))]
    tail = jnp.where(lanes < third, thirds[0], jnp.where(lanes < 2 * third, thirds[1], thirds[2]))
    return jnp.concatenate([first, second, tail], axis=0)


def fold(values, row):
    values = list(values) + [None] * (8 - len(values))
    for half in (4, 2, 1):
        upper = jnp.bitwise_and(row, half) != 0
        values = [fold_two(one, two, half, upper) for one, two in zip(values[0::2], values[1::2])]
    return values[0]


def fold_two(one, two, half, upper):
    if one is None:
        return None
    if two is None:
        return one + across(one, half, upper)
    return jnp.where(upper, two, one) + across(jnp.where(upper, one, two), half, upper)


def across(x, half, upper):
    if half == 4:
        return pltpu.roll(x, 4, 0)
    return jnp.where(upper, pltpu.roll(x, half, 0), pltpu.roll(x, 8 - half, 0))


def shuffle(x, index):
    return lax.gather(
        x,
        index[:, :, None],
        lax.GatherDimensionNumbers(
            offset_dims=(),
            collapsed_slice_dims=(0,),
            start_index_map=(0,),
            operand_batching_dims=(1,),
            start_indices_batching_dims=(1,),
        ),
        slice_sizes=(1, 1),
        mode=lax.GatherScatterMode.PROMISE_IN_BOUNDS,
    )


def rows_of(wanted, row):
    out = jnp.zeros(row.shape, jnp.int32)
    for s, value in enumerate(wanted):
        out = jnp.where(row == s, value, out)
    return out


def gram_kernel(shares, count, *refs):
    own_ref, index_ref, weight_ref, ids_ref, picked_ref = refs[:5]
    others, starts = refs[5 : 5 + count], refs[5 + count : 5 + 2 * count]
    out_ref, *table_refs = refs[5 + 2 * count :]
    vectors, rows = own_ref.shape
    pairs = pair_list(vectors)
    padded = 24
    tables = []
    for other_ref, start_ref, table_ref in zip(others, starts, table_refs):
        table_ref[...] = encode(other_ref[...])
        tables.append((table_ref, start_ref[0]))
    words = picked_ref.shape[0]
    half_shares = shares // 2
    gram = [jnp.zeros((half_shares * 2 * padded, AGG_DEV), jnp.float32) for _ in range(4)]
    step = LANES
    rows8 = lax.broadcasted_iota(jnp.int32, (8, LANES), 0)
    place = [4 * (v & 1) + (v & 2) + (v >> 2) for v in range(8)]
    unit = jnp.where(rows_of(place, rows8) < words, 1.0 / SCALE_WHOLE, 1.0 / SCALE_SPLIT)
    order = rows_of([place.index(s) for s in range(8)], rows8)
    listed = pairs + [(0, 0)] * (padded - len(pairs))
    sides = [
        tuple(rows_of([place[pair[side]] for pair in listed[at : at + 8]], rows8) for side in range(2))
        for at in range(0, padded, 8)
    ]
    for first in range(0, rows, step):
        here = slice(first, first + step)
        picked = pick([picked_ref[word, :, here] for word in range(words)], index_ref[:, here], tables)
        near = fold([weight_ref[:, here] * value for value in decode(picked)], rows8) * unit
        own = jnp.concatenate([own_ref[:, here], jnp.zeros((8 - vectors, step), jnp.float32)], axis=0)
        smooth = shuffle(own, order) - near
        terms = jnp.concatenate([shuffle(smooth, p) * shuffle(smooth, q) for p, q in sides], axis=0)
        coarse = terms.astype(jnp.bfloat16).astype(jnp.float32)
        both = jnp.concatenate([coarse, terms - coarse], axis=0)
        share = jnp.broadcast_to(share_of(ids_ref[:, first : first + step], shares), (2 * padded, step))
        ids = ids_ref[:, first : first + step]
        within = ids - share[:1] * AGG_DEV
        columns = lax.broadcasted_iota(jnp.int32, (AGG_DEV, step), 0)
        one_hot = (columns == within).astype(jnp.float32).astype(jnp.bfloat16)
        for half in range(2):
            masked = jnp.concatenate(
                [jnp.where(share == half * half_shares + s, both, 0.0) for s in range(half_shares)], axis=0
            ).astype(jnp.bfloat16)
            turn = 2 * (first // step % 2) + half
            gram[turn] = gram[turn] + lax.dot_general(
                masked,
                one_hot,
                (((1,), (1,)), ((), ())),
                preferred_element_type=jnp.float32,
            )
    gram = [gram[half] + gram[2 + half] for half in range(2)]
    for half in range(2):
        for s in range(half_shares):
            at = 2 * padded * s
            out_ref[half * half_shares + s] = to_wire(
                gram[half][at : at + padded] + gram[half][at + padded : at + 2 * padded]
            )


def factor_kernel(vectors, parts_ref, factor_ref, spread_ref):
    pairs = pair_list(vectors)
    sums = [parts_ref[source] for source in range(parts_ref.shape[0])]
    while len(sums) > 1:
        odd = sums[len(sums) // 2 * 2 :]
        sums = [one + two for one, two in zip(sums[0::2], sums[1::2])] + odd
    total = from_wire(sums[0])[:, :AGG_DEV]
    entry = {}
    for i, (p, q) in enumerate(pairs):
        value = total[i : i + 1] * (AGG_DEV / ROWS_DEV)
        entry[p, q] = value + 1.0 if p == q else value
    upper = {}
    for j in range(vectors):
        pivot = entry[j, j]
        for k in range(j):
            pivot = pivot - upper[k, j] * upper[k, j]
        inverse = lax.rsqrt(pivot)
        upper[j, j] = pivot * inverse
        for i in range(j + 1, vectors):
            rest = entry[j, i]
            for k in range(j):
                rest = rest - upper[k, i] * upper[k, j]
            upper[j, i] = rest * inverse
    for i, pair in enumerate(pairs):
        factor_ref[i : i + 1, :] = upper[pair]
    most = functools.reduce(jnp.maximum, [upper[j, j] for j in range(vectors)])
    least = functools.reduce(jnp.minimum, [upper[j, j] for j in range(vectors)])
    spread_ref[...] = jnp.log(most) - jnp.log(least)


def shards(nullspace, agg_ids, nbr_index, nbr_weight):
    vectors, rows = nullspace.shape
    assert vectors % 3 == 0 and rows % (2 * LANES) == 0
    words = 2 * vectors // 3
    groups, shares = lax.axis_size("grp"), lax.axis_size("blk")
    pairs = pair_list(vectors)
    assert len(pairs) == 21 and shares % 2 == 0
    vmem = pl.BlockSpec(memory_space=pltpu.VMEM)
    smem = pl.BlockSpec(memory_space=pltpu.SMEM)
    if groups == 2:
        others = [lax.ppermute(nullspace, "grp", [(0, 1), (1, 0)])]
        group = jnp.bitwise_xor(lax.axis_index("grp").astype(jnp.int32), 6) * 3
        for n in range(PARITY_STEPS):
            group = group * 3 + 2 * (n + 1)
        group = jnp.bitwise_and(group, 1)
        starts = [(2 * rows * (1 - group)).reshape(1)]
    else:
        others = [
            lax.ppermute(nullspace, "grp", [(i, i + 1) for i in range(groups - 1)]),
            lax.ppermute(nullspace, "grp", [(i + 1, i) for i in range(groups - 1)]),
        ]
        starts = [jnp.zeros((1,), jnp.int32), jnp.full((1,), 2 * rows, jnp.int32)]
    ids = agg_ids.reshape(1, rows)
    picked = pl.pallas_call(
        own_kernel,
        out_shape=jax.ShapeDtypeStruct((words,) + nbr_index.shape, jnp.int32),
        in_specs=[vmem, vmem],
        out_specs=vmem,
        scratch_shapes=[pltpu.VMEM((words, rows), jnp.int32)],
        compiler_params=pltpu.CompilerParams(vmem_limit_bytes=4 << 20),
        cost_estimate=pl.CostEstimate(flops=1 << 22, bytes_accessed=1 << 18, transcendentals=0),
        name="own",
    )(nullspace, nbr_index)
    partial = pl.pallas_call(
        functools.partial(gram_kernel, shares, len(others)),
        out_shape=jax.ShapeDtypeStruct((shares, 16, LANES), jnp.float32),
        in_specs=[vmem] * (5 + len(others)) + [smem] * len(others),
        out_specs=vmem,
        scratch_shapes=[pltpu.VMEM((words, rows), jnp.int32) for _ in others],
        compiler_params=pltpu.CompilerParams(vmem_limit_bytes=8 << 20),
        name="gram",
    )(nullspace, nbr_index, nbr_weight, ids, picked, *others, *starts)
    parts = lax.all_to_all(partial, "blk", 0, 0, tiled=True)
    factor, spread = pl.pallas_call(
        functools.partial(factor_kernel, vectors),
        out_shape=(
            jax.ShapeDtypeStruct((len(pairs), AGG_DEV), jnp.float32),
            jax.ShapeDtypeStruct((1, AGG_DEV), jnp.float32),
        ),
        in_specs=[vmem],
        out_specs=(vmem, vmem),
        compiler_params=pltpu.CompilerParams(vmem_limit_bytes=4 << 20),
        name="factor",
    )(parts)
    return factor, spread.reshape(AGG_DEV)


def solution(mesh):
    return jax.shard_map(
        shards,
        mesh=mesh,
        in_specs=(
            P(None, ("grp", "blk")),
            P(("grp", "blk")),
            P(None, ("grp", "blk")),
            P(None, ("grp", "blk")),
        ),
        out_specs=(P(None, ("grp", "blk")), P(("grp", "blk"))),
        check_vma=False,
    )
```

```python
import functools

import jax
import jax.numpy as jnp
from jax import lax
from jax.experimental import pallas as pl
from jax.experimental.pallas import tpu as pltpu
from jax.sharding import PartitionSpec as P

ROWS_DEV = 2048
AGG_DEV = 96
LANES = 128
NULL_MOST = 6.0
SPLIT = 11
SCALE_WHOLE = (2.0 ** (31 - SPLIT) - 1.0) / NULL_MOST
SCALE_SPLIT = (2.0 ** (2 * SPLIT - 1) - 1.0) / NULL_MOST
KEEP = (1 << SPLIT) - 1
PARITY_STEPS = 30


def pair_list(vectors):
    return [(p, q) for p in range(vectors) for q in range(p, vectors)]


def share_of(ids, shares):
    shift = 22
    factor = -(-(1 << shift) // AGG_DEV)
    most = shares * AGG_DEV - 1
    assert most * factor < 2**31 and (factor * AGG_DEV - (1 << shift)) * most < (1 << shift)
    return lax.shift_right_logical(ids * factor, shift)


def encode(table):
    words = 2 * table.shape[0] // 3
    whole = jnp.round(table[:words] * SCALE_WHOLE).astype(jnp.int32)
    split = jnp.round(table[words:] * SCALE_SPLIT).astype(jnp.int32)
    lower = [
        jnp.bitwise_and(split[r // 2 : r // 2 + 1] >> (0 if r % 2 else SPLIT), KEEP) for r in range(words)
    ]
    return jnp.bitwise_or(whole << SPLIT, jnp.concatenate(lower, axis=0))


def decode(words):
    values = [(word >> SPLIT).astype(jnp.float32) for word in words]
    for upper, lower in zip(words[0::2], words[1::2]):
        split = jnp.bitwise_or((upper << (32 - SPLIT)) >> (32 - 2 * SPLIT), jnp.bitwise_and(lower, KEEP))
        values.append(split.astype(jnp.float32))
    return values


def lane_pick(rows, low):
    return lax.gather(
        rows,
        low[:, :, None],
        lax.GatherDimensionNumbers(
            offset_dims=(),
            collapsed_slice_dims=(1,),
            start_index_map=(1,),
            operand_batching_dims=(0,),
            start_indices_batching_dims=(0,),
        ),
        slice_sizes=(1, 1),
        mode=lax.GatherScatterMode.PROMISE_IN_BOUNDS,
    )


def pick(picked, index, tables, first=0):
    low = jnp.bitwise_and(index, LANES - 1)
    for table_ref, base in tables:
        high = lax.shift_right_arithmetic(index - base, LANES.bit_length() - 1)
        for chunk in range(table_ref.shape[1] // LANES):
            found = high == chunk
            for word in range(len(picked)):
                row = table_ref[first + word : first + word + 1, chunk * LANES : (chunk + 1) * LANES]
                value = lane_pick(jnp.broadcast_to(row, index.shape), low)
                picked[word] = jnp.where(found, value, picked[word])
    return picked


def own_kernel(own_ref, index_ref, picked_ref, table_ref):
    rows = own_ref.shape[1]
    table_ref[...] = encode(own_ref[...])
    for start in range(0, rows, LANES):
        here = slice(start, start + LANES)
        index = index_ref[:, here]
        for word in range(0, table_ref.shape[0], 2):
            zero = [jnp.zeros(index.shape, jnp.int32) for _ in range(2)]
            found = pick(zero, index, [(table_ref, rows)], word)
            for i, value in enumerate(found):
                picked_ref[word + i, :, here] = value


def to_wire(gram):
    tail = jnp.concatenate([gram[16:], jnp.zeros((8, LANES - AGG_DEV), gram.dtype)], axis=1)
    lanes = lax.broadcasted_iota(jnp.int32, (8, LANES), 1)
    rows = lax.broadcasted_iota(jnp.int32, (8, LANES), 0)
    out = []
    third = AGG_DEV // 3
    thirds = [pltpu.roll(tail, AGG_DEV - third * i, 1) for i in range(3)]
    for half in range(2):
        main = jnp.concatenate(
            [gram[8 * half : 8 * half + 8], jnp.zeros((8, LANES - AGG_DEV), gram.dtype)], axis=1
        )
        last = pltpu.roll(thirds[2], 5 - 3 * half, 0)
        side = jnp.where(rows < 5, thirds[half], last)
        out.append(jnp.where(lanes < AGG_DEV, main, side))
    return jnp.concatenate(out, axis=0)


def from_wire(wire):
    third = AGG_DEV // 3
    lanes = lax.broadcasted_iota(jnp.int32, (8, LANES), 1)
    rows = lax.broadcasted_iota(jnp.int32, (8, LANES), 0)
    first, second = wire[:8], wire[8:]
    last = jnp.where(rows < 3, pltpu.roll(first, 3, 0), pltpu.roll(second, 6, 0))
    thirds = [pltpu.roll(x, LANES - AGG_DEV + third * i, 1) for i, x in enumerate((first, second, last))]
    tail = jnp.where(lanes < third, thirds[0], jnp.where(lanes < 2 * third, thirds[1], thirds[2]))
    return jnp.concatenate([first, second, tail], axis=0)


def fold(values, row):
    values = list(values) + [None] * (8 - len(values))
    for half in (4, 2, 1):
        upper = jnp.bitwise_and(row, half) != 0
        values = [fold_two(one, two, half, upper) for one, two in zip(values[0::2], values[1::2])]
    return values[0]


def fold_two(one, two, half, upper):
    if one is None:
        return None
    if two is None:
        return one + across(one, half, upper)
    return jnp.where(upper, two, one) + across(jnp.where(upper, one, two), half, upper)


def across(x, half, upper):
    if half == 4:
        return pltpu.roll(x, 4, 0)
    return jnp.where(upper, pltpu.roll(x, half, 0), pltpu.roll(x, 8 - half, 0))


def shuffle(x, index):
    return lax.gather(
        x,
        index[:, :, None],
        lax.GatherDimensionNumbers(
            offset_dims=(),
            collapsed_slice_dims=(0,),
            start_index_map=(0,),
            operand_batching_dims=(1,),
            start_indices_batching_dims=(1,),
        ),
        slice_sizes=(1, 1),
        mode=lax.GatherScatterMode.PROMISE_IN_BOUNDS,
    )


def rows_of(wanted, row):
    out = jnp.zeros(row.shape, jnp.int32)
    for s, value in enumerate(wanted):
        out = jnp.where(row == s, value, out)
    return out


def gram_kernel(shares, count, *refs):
    own_ref, index_ref, weight_ref, ids_ref, picked_ref = refs[:5]
    others, starts = refs[5 : 5 + count], refs[5 + count : 5 + 2 * count]
    out_ref, *table_refs = refs[5 + 2 * count :]
    vectors, rows = own_ref.shape
    pairs = pair_list(vectors)
    padded = 24
    tables = []
    for other_ref, start_ref, table_ref in zip(others, starts, table_refs):
        table_ref[...] = encode(other_ref[...])
        tables.append((table_ref, start_ref[0]))
    words = picked_ref.shape[0]
    half_shares = shares // 2
    gram = [jnp.zeros((half_shares * 2 * padded, AGG_DEV), jnp.float32) for _ in range(4)]
    step = LANES
    rows8 = lax.broadcasted_iota(jnp.int32, (8, LANES), 0)
    place = [4 * (v & 1) + (v & 2) + (v >> 2) for v in range(8)]
    unit = jnp.where(rows_of(place, rows8) < words, 1.0 / SCALE_WHOLE, 1.0 / SCALE_SPLIT)
    order = rows_of([place.index(s) for s in range(8)], rows8)
    listed = pairs + [(0, 0)] * (padded - len(pairs))
    sides = [
        tuple(rows_of([place[pair[side]] for pair in listed[at : at + 8]], rows8) for side in range(2))
        for at in range(0, padded, 8)
    ]
    for first in range(0, rows, step):
        here = slice(first, first + step)
        picked = pick([picked_ref[word, :, here] for word in range(words)], index_ref[:, here], tables)
        near = fold([weight_ref[:, here] * value for value in decode(picked)], rows8) * unit
        own = jnp.concatenate([own_ref[:, here], jnp.zeros((8 - vectors, step), jnp.float32)], axis=0)
        smooth = shuffle(own, order) - near
        terms = jnp.concatenate([shuffle(smooth, p) * shuffle(smooth, q) for p, q in sides], axis=0)
        coarse = terms.astype(jnp.bfloat16).astype(jnp.float32)
        both = jnp.concatenate([coarse, terms - coarse], axis=0)
        share = jnp.broadcast_to(share_of(ids_ref[:, first : first + step], shares), (2 * padded, step))
        ids = ids_ref[:, first : first + step]
        within = ids - share[:1] * AGG_DEV
        columns = lax.broadcasted_iota(jnp.int32, (AGG_DEV, step), 0)
        one_hot = (columns == within).astype(jnp.float32).astype(jnp.bfloat16)
        for half in range(2):
            masked = jnp.concatenate(
                [jnp.where(share == half * half_shares + s, both, 0.0) for s in range(half_shares)], axis=0
            ).astype(jnp.bfloat16)
            turn = 2 * (first // step % 2) + half
            gram[turn] = gram[turn] + lax.dot_general(
                masked,
                one_hot,
                (((1,), (1,)), ((), ())),
                preferred_element_type=jnp.float32,
            )
    gram = [gram[half] + gram[2 + half] for half in range(2)]
    for half in range(2):
        for s in range(half_shares):
            at = 2 * padded * s
            out_ref[half * half_shares + s] = to_wire(
                gram[half][at : at + padded] + gram[half][at + padded : at + 2 * padded]
            )


def factor_kernel(vectors, parts_ref, factor_ref, spread_ref):
    pairs = pair_list(vectors)
    sums = [parts_ref[source] for source in range(parts_ref.shape[0])]
    while len(sums) > 1:
        odd = sums[len(sums) // 2 * 2 :]
        sums = [one + two for one, two in zip(sums[0::2], sums[1::2])] + odd
    total = from_wire(sums[0] * (AGG_DEV / ROWS_DEV))[:, :AGG_DEV]
    entry = {}
    for i, (p, q) in enumerate(pairs):
        value = total[i : i + 1]
        entry[p, q] = value + 1.0 if p == q else value
    upper = {}
    for j in range(vectors):
        pivot = entry[j, j]
        for k in range(j):
            pivot = pivot - upper[k, j] * upper[k, j]
        inverse = lax.rsqrt(pivot)
        upper[j, j] = pivot * inverse
        for i in range(j + 1, vectors):
            rest = entry[j, i]
            for k in range(j):
                rest = rest - upper[k, i] * upper[k, j]
            upper[j, i] = rest * inverse
    for i, pair in enumerate(pairs):
        factor_ref[i : i + 1, :] = upper[pair]
    most = functools.reduce(jnp.maximum, [upper[j, j] for j in range(vectors)])
    least = functools.reduce(jnp.minimum, [upper[j, j] for j in range(vectors)])
    spread_ref[...] = jnp.log(most) - jnp.log(least)


def shards(nullspace, agg_ids, nbr_index, nbr_weight):
    vectors, rows = nullspace.shape
    assert vectors % 3 == 0 and rows % (2 * LANES) == 0
    words = 2 * vectors // 3
    groups, shares = lax.axis_size("grp"), lax.axis_size("blk")
    pairs = pair_list(vectors)
    assert len(pairs) == 21 and shares % 2 == 0
    vmem = pl.BlockSpec(memory_space=pltpu.VMEM)
    smem = pl.BlockSpec(memory_space=pltpu.SMEM)
    if groups == 2:
        others = [lax.ppermute(nullspace, "grp", [(0, 1), (1, 0)])]
        group = jnp.bitwise_xor(lax.axis_index("grp").astype(jnp.int32), 6) * 3
        for n in range(PARITY_STEPS):
            group = group * 3 + 2 * (n + 1)
        group = jnp.bitwise_and(group, 1)
        starts = [(2 * rows * (1 - group)).reshape(1)]
    else:
        others = [
            lax.ppermute(nullspace, "grp", [(i, i + 1) for i in range(groups - 1)]),
            lax.ppermute(nullspace, "grp", [(i + 1, i) for i in range(groups - 1)]),
        ]
        starts = [jnp.zeros((1,), jnp.int32), jnp.full((1,), 2 * rows, jnp.int32)]
    ids = agg_ids.reshape(1, rows)
    picked = pl.pallas_call(
        own_kernel,
        out_shape=jax.ShapeDtypeStruct((words,) + nbr_index.shape, jnp.int32),
        in_specs=[vmem, vmem],
        out_specs=vmem,
        scratch_shapes=[pltpu.VMEM((words, rows), jnp.int32)],
        compiler_params=pltpu.CompilerParams(vmem_limit_bytes=4 << 20),
        cost_estimate=pl.CostEstimate(flops=1 << 22, bytes_accessed=1 << 18, transcendentals=0),
        name="own",
    )(nullspace, nbr_index)
    partial = pl.pallas_call(
        functools.partial(gram_kernel, shares, len(others)),
        out_shape=jax.ShapeDtypeStruct((shares, 16, LANES), jnp.float32),
        in_specs=[vmem] * (5 + len(others)) + [smem] * len(others),
        out_specs=vmem,
        scratch_shapes=[pltpu.VMEM((words, rows), jnp.int32) for _ in others],
        compiler_params=pltpu.CompilerParams(vmem_limit_bytes=8 << 20),
        name="gram",
    )(nullspace, nbr_index, nbr_weight, ids, picked, *others, *starts)
    parts = lax.all_to_all(partial, "blk", 0, 0, tiled=True)
    factor, spread = pl.pallas_call(
        functools.partial(factor_kernel, vectors),
        out_shape=(
            jax.ShapeDtypeStruct((len(pairs), AGG_DEV), jnp.float32),
            jax.ShapeDtypeStruct((1, AGG_DEV), jnp.float32),
        ),
        in_specs=[vmem],
        out_specs=(vmem, vmem),
        compiler_params=pltpu.CompilerParams(vmem_limit_bytes=4 << 20),
        name="factor",
    )(parts)
    return factor, spread.reshape(AGG_DEV)


def solution(mesh):
    return jax.shard_map(
        shards,
        mesh=mesh,
        in_specs=(
            P(None, ("grp", "blk")),
            P(("grp", "blk")),
            P(None, ("grp", "blk")),
            P(None, ("grp", "blk")),
        ),
        out_specs=(P(None, ("grp", "blk")), P(("grp", "blk"))),
        check_vma=False,
    )
```
